256 devices in a mesh: space: 8 (over z), work: 32 (over y, x, core).
Axes of the slice: x: 4, y: 4, z: 8, core: 2. Of those that a mesh axis runs over, the one named last changes fastest.
Arguments:
- positions: float32 [3, 262144], P(None, ('space', 'work')), may hold values from -3 to 3
- velocities: float32 [3, 262144], P(None, ('space', 'work')), may hold values from -2 to 2
- masses: float32 [262144], P(('space', 'work')), may hold values from 0.001 to 0.01
- sound2: float32 [262144], P(('space', 'work')), may hold values from 0.1 to 1
- ghost_list: int32 [1024, 2], P(('space', 'work')), may hold values from 0 to 7
- dens_list: int32 [2048, 6], P(('space', 'work')), may hold values from 0 to 15
- pair_dest: int32 [16384, 1], P(('space', 'work')), may hold values from 0 to 31; in each aligned block of 64 rows (0 to 63, 64 to 127, ...) at most 4 rows name the same one
- pair_tiles: int32 [16384, 2], P(('space', 'work')), may hold values from 0 to 7
Outputs:
- new_positions: float32 [3, 262144], P(None, ('space', 'work'))
- new_velocities: float32 [3, 262144], P(None, ('space', 'work'))
- acceleration: float32 [3, 262144], P(None, ('space', 'work'))
- density: float32 [262144], P(('space', 'work'))
The draws below stay inside these ranges and needn't reach their ends.
Inputs may be any that keep to these rules, and one draw needn't show every extreme that they name: `pair_dest`: at most 4 pairs of one device name the same owner; in every draw some device has exactly 4 pairs for one owner.
All inputs are finite; a program needn't handle non-finite values.
Results may differ from the reference program's by a relative error of at most 0.0001.
Values sent between devices are 32-bit elements; how exact they have to be, the bound alone decides.
No kernel may reach another device: no remote copies, remote signals or barrier semaphores. Data moves between devices by JAX's collectives and lax.ppermute only.
A program may use at most 64 MiB of HBM per device.

```python
import math
import jax
import jax.numpy as jnp
import numpy as np
from jax import lax

TD = 8
G = 4
NBD = 6
PAIRS_DEV = 64
CAP = 4
STEPS = 2
TILES = 2048
NPART = 262144
PAIRS = 16384
GHOSTS = 1024
N_SPACE = 8
N_WORK = 32


def set_ends(array, own_key, low, high):
    dims = array.shape
    spot = [jax.random.randint(jax.random.fold_in(own_key, axis), (), 0, dims[axis]) for axis in range(len(dims))]
    array = array.at[tuple(spot)].set(low)
    longest = dims.index(max(dims))
    spot[longest] = (spot[longest] + 1) % dims[longest]
    return array.at[tuple(spot)].set(high)


def block_scale(stream_key, extent, pieces, least, largest):
    def one(dim, parts):
        steps = jax.random.uniform(jax.random.fold_in(jax.random.fold_in(stream_key, 6), dim), (parts,), jnp.float32, least / len(pieces), largest / len(pieces))
        return jnp.repeat(jnp.exp(steps), extent[dim] // parts).reshape((-1,) + (1,) * (len(extent) - dim - 1))

    loudness = one(*pieces[0])
    for cut in pieces[1:]:
        loudness = loudness * one(*cut)
    return loudness


def assign_block(rng, own, number, rows, number_of, top, limit, lean):
    ranking = jax.random.permutation(rng, number_of)
    crowded, usual = shares(number_of, rows * top, limit, lean, True), shares(number_of, rows * top, limit, lean, False)
    places = jnp.arange(number_of)

    def named(tallies, turn):
        used = int((tallies > 0).sum())
        fixed = max(1, used // 4)
        passed = fixed + (places - fixed + turn * (used - fixed)) % max(1, number_of - fixed)
        return jnp.zeros((number_of,), jnp.int32).at[ranking[jnp.where(places < fixed, places, passed)]].set(jnp.asarray(tallies, jnp.int32))

    tallies = jnp.where(number % 4 == 0, named(crowded, number // 4), named(usual, number - number // 4 - 1))
    mixed = jax.random.permutation(jax.random.fold_in(own, 3), number_of)
    source_of, taker = mixed[0:number_of // 2 * 2:2], mixed[1:number_of // 2 * 2:2]
    room = jnp.minimum(tallies[source_of] - 1, limit - tallies[taker]) // 2
    room = jnp.where((source_of == ranking[0]) | (taker == ranking[0]) | (tallies[taker] == 0), 0, jnp.maximum(room, 0))
    passed = jax.random.randint(jax.random.fold_in(own, 4), (number_of // 2,), 0, 1 << 20) % (room + 1)
    tallies = tallies.at[source_of].add(-passed).at[taker].add(passed)
    members = jnp.searchsorted(jnp.cumsum(tallies), jnp.arange(rows * top), side="right").astype(jnp.int32)
    table = members.reshape(top, rows).T
    table = table[jax.random.permutation(jax.random.fold_in(own, 1), rows)]
    turn = jax.random.randint(jax.random.fold_in(own, 2), (rows, 1), 0, top)
    return jnp.take_along_axis(table, (jnp.arange(top)[None, :] + turn) % top, axis=1)


def shares(amount, total, limit, skew, full):
    loads = [(1 << 20) // math.isqrt(rank ** skew) + 1 for rank in range(1, amount + 1)]
    largest = limit if full else min(limit, max(-(-total // amount), total * loads[0] // sum(loads)))
    least = 1 if total - largest >= amount - 1 else 0
    holding, surplus = [largest] + [least] * (amount - 1), total - largest - least * (amount - 1)
    while surplus > 0:
        free = [i for i in range(1, amount) if holding[i] < largest] or [i for i in range(1, amount) if holding[i] < limit]
        pool, left = sum([loads[i] for i in free]), surplus
        for i in free:
            addition = min(limit - holding[i], max(1, left * loads[i] // pool), surplus)
            holding[i] = holding[i] + addition
            surplus = surplus - addition
    return np.array(holding)


def scatter_about(stream_key, shape, spread, most, pieces=(), held_as=jnp.bfloat16):
    entries = jax.random.normal(stream_key, shape, jnp.float32) * spread
    if len(pieces) > 0:
        entries = block_scale(stream_key, shape, pieces, -0.22, 0.18) * entries
    return jnp.clip(entries, min=-most, max=most).astype(held_as)


def setup_inputs(seed: int = 0) -> dict:
    splits = jax.random.split(jax.random.key(seed), 9)
    positions = scatter_about(splits[0], (3, NPART), 0.5, 3.0, ((1, 256),), jnp.float32)
    velocities = scatter_about(splits[1], (3, NPART), 0.3, 2.0, ((1, 256),), jnp.float32)
    masses = jnp.clip(jnp.exp(math.log(0.01) - 2.30258502 * jax.random.uniform(splits[2], (NPART,), jnp.float32) ** block_scale(splits[2], (NPART,), ((0, 256),), -0.2, 0.2)), 0.001, 0.01)
    sound2 = jnp.clip(jnp.exp(math.log(1.0) - 2.3025851 * jax.random.uniform(splits[3], (NPART,), jnp.float32) ** block_scale(splits[3], (NPART,), ((0, 256),), -0.2, 0.2)), 0.1, 1.0)
    ghost_list = set_ends(jax.random.randint(splits[4], (GHOSTS, 2), 0, TD), jax.random.fold_in(splits[4], 1), 0, TD - 1).astype(jnp.int32)
    dens_list = set_ends(jax.random.randint(splits[5], (TILES, NBD), 0, TD + 2 * G), jax.random.fold_in(splits[5], 1), 0, (TD + 2 * G) - 1).astype(jnp.int32)
    pair_dest_keys = jax.random.split(jax.random.fold_in(splits[6], 1), PAIRS // PAIRS_DEV)
    pair_dest_turns = jax.random.permutation(jax.random.fold_in(splits[6], 3), PAIRS // PAIRS_DEV)
    pair_dest = jax.vmap(lambda own, number: assign_block(jax.random.fold_in(splits[6], 2), own, number, PAIRS_DEV, N_WORK, 1, CAP, 2))(pair_dest_keys, pair_dest_turns).reshape((PAIRS, 1))
    pair_tiles = set_ends(jax.random.randint(splits[7], (PAIRS, 2), 0, TD), jax.random.fold_in(splits[7], 1), 0, TD - 1).astype(jnp.int32)
    return {"positions": positions, "velocities": velocities, "masses": masses, "sound2": sound2, "ghost_list": ghost_list, "dens_list": dens_list, "pair_dest": pair_dest, "pair_tiles": pair_tiles}


kernel_scale = 1.0
viscous_alpha = 1.0
viscous_beta = 2.0
star_mass = 0.5
softening = 0.1
time_step = 0.1

def tile_density(home_tile, neighbours):
    combined = jnp.concatenate([home_tile[None], neighbours], axis=0)
    combined = jnp.transpose(combined, (1, 0, 2)).reshape(4, -1)
    distance2 = jnp.zeros((home_tile.shape[1], combined.shape[1]), jnp.float32)
    for k in range(3):
        offset = home_tile[k][:, None] - combined[k][None, :]
        distance2 = distance2 + offset * offset
    kernel = jnp.exp(-distance2 * kernel_scale)
    return lax.optimization_barrier(jnp.sum(kernel * combined[3][None, :], axis=1))

def pair_terms(first_tile, second_tile):
    offsets = first_tile[0:3, :, None] - second_tile[0:3, None, :]
    distance2 = lax.optimization_barrier(jnp.sum(offsets * offsets, axis=0))
    velocity_gap = first_tile[3:6, :, None] - second_tile[3:6, None, :]
    approach = lax.optimization_barrier(jnp.sum(velocity_gap * offsets, axis=0))
    closing = jnp.minimum(approach / (distance2 + 0.01), 0.0)
    mean_sound = 0.5 * (first_tile[9][:, None] + second_tile[9][None, :])
    mean_density = 0.5 * (first_tile[7][:, None] + second_tile[7][None, :])
    viscous = (-viscous_alpha * mean_sound * closing + viscous_beta * closing * closing) / mean_density
    strength = first_tile[8][:, None] + second_tile[8][None, :] + viscous
    weight = strength * jnp.exp(-distance2 * kernel_scale) * (2.0 * kernel_scale)
    on_first = lax.optimization_barrier(jnp.sum(weight[None] * second_tile[6][None, None, :] * offsets, axis=2))
    on_second = -lax.optimization_barrier(jnp.sum(weight[None] * first_tile[6][None, :, None] * offsets, axis=1))
    return (on_first, on_second)

def star_pull(positions):
    radius2 = lax.optimization_barrier(jnp.sum(positions * positions, axis=0)) + softening
    return -star_mass * positions / (radius2 * jnp.sqrt(radius2))[None, :]

def reference(positions, velocities, masses, sound2, ghost_list, dens_list, pair_dest, pair_tiles):
    device_total = N_SPACE * N_WORK
    tile_total = device_total * TD
    pair_total = device_total * PAIRS_DEV
    per_block = 16
    device_ids = jnp.arange(device_total, dtype=jnp.int32)
    sector = device_ids // N_WORK
    work_place = device_ids % N_WORK
    lower_device = (sector - 1) % N_SPACE * N_WORK + work_place
    upper_device = (sector + 1) % N_SPACE * N_WORK + work_place
    ghosts = ghost_list.reshape(device_total, G, 2)
    own_ids = device_ids[:, None] * TD + jnp.arange(TD, dtype=jnp.int32)[None, :]
    from_below = lower_device[:, None] * TD + ghosts[lower_device][:, :, 0]
    from_above = upper_device[:, None] * TD + ghosts[upper_device][:, :, 1]
    candidates = jnp.concatenate([own_ids, from_below, from_above], axis=1)
    tile_device = jnp.arange(tile_total, dtype=jnp.int32) // TD
    density_tiles = candidates[tile_device[:, None], dens_list]
    pair_device = jnp.arange(pair_total, dtype=jnp.int32) // PAIRS_DEV
    first_ids = pair_device * TD + pair_tiles[:, 0]
    second_ids = (pair_device - pair_device % N_WORK + pair_dest[:, 0]) * TD + pair_tiles[:, 1]
    tile_mass = masses.reshape(tile_total, 1, 128)
    sound_speed = jnp.sqrt(sound2).reshape(tile_total, 1, 128)
    acceleration = jnp.zeros_like(positions)
    density = jnp.zeros_like(masses)
    for _ in range(STEPS):
        tile_pos = jnp.transpose(positions.reshape(3, tile_total, 128), (1, 0, 2))
        tile_vel = jnp.transpose(velocities.reshape(3, tile_total, 128), (1, 0, 2))
        source = jnp.concatenate([tile_pos, tile_mass], axis=1)

        def density_block(indices):
            return jax.vmap(tile_density)(source[indices[0]], source[indices[1]])
        density = lax.map(density_block, (jnp.arange(tile_total, dtype=jnp.int32).reshape(-1, per_block), density_tiles.reshape(-1, per_block, NBD))).reshape(-1)
        pressure_term = (sound2 / density).reshape(tile_total, 1, 128)
        payload = jnp.concatenate([tile_pos, tile_vel, tile_mass, density.reshape(tile_total, 1, 128), pressure_term, sound_speed], axis=1)

        def pair_block(indices):
            return jax.vmap(pair_terms)(payload[indices[0]], payload[indices[1]])
        on_first, on_second = lax.map(pair_block, (first_ids.reshape(-1, per_block), second_ids.reshape(-1, per_block)))
        pair_gains = jnp.zeros((tile_total, 3, 128), jnp.float32)
        pair_gains = pair_gains.at[first_ids].add(on_first.reshape(-1, 3, 128))
        pair_gains = pair_gains.at[second_ids].add(on_second.reshape(-1, 3, 128))
        acceleration = jnp.transpose(pair_gains, (1, 0, 2)).reshape(3, -1) + star_pull(positions)
        velocities = velocities + time_step * acceleration
        positions = positions + time_step * velocities
    return (positions, velocities, acceleration, density)
```

```python
import jax
import jax.numpy as jnp
from jax import lax
from jax.experimental import pallas as pl
from jax.experimental.pallas import tpu as pltpu
from jax.sharding import Mesh, PartitionSpec as P

TD = 8
G = 4
NBD = 6
CAP = 4
PAIRS = 64
CHIPS = 16
OTHERS = 2 * CHIPS * TD
LOG2E = 1.4426950408889634
STAR = 0.5
SOFT = 0.1
DT = 0.1

VMEM = pl.BlockSpec(memory_space=pltpu.VMEM)
SMEM = pl.BlockSpec(memory_space=pltpu.SMEM)


def f32(*shape):
    return jax.ShapeDtypeStruct(shape, jnp.float32)


def i32(*shape):
    return jax.ShapeDtypeStruct(shape, jnp.int32)


def ghosts_kernel(pos, mass, ghost, to_next, to_prev):
    for side, out in enumerate((to_next, to_prev)):
        for j in range(G):
            t = ghost[side, j]
            out[4 * j : 4 * j + 3, :] = pos[:, pl.ds(pl.multiple_of(t * 128, 128), 128)]
            out[4 * j + 3 : 4 * j + 4, :] = mass[pl.ds(t, 1), :]


def routes_kernel(dest, tiles, codes, table):
    core = lax.axis_index("core")
    d = dest[...]
    t0 = tiles[0:1, :]
    t1 = tiles[1:2, :]
    half = (d % 2) ^ core
    codes[...] = t0 * 256 + half * (CHIPS * TD) + (d // 2) * TD + t1
    place = lax.broadcasted_iota(jnp.int32, (2 * CHIPS, PAIRS), 0)
    hits = (place == d).astype(jnp.float32)
    earlier = (
        lax.broadcasted_iota(jnp.int32, (PAIRS, PAIRS), 0)
        < lax.broadcasted_iota(jnp.int32, (PAIRS, PAIRS), 1)
    ).astype(jnp.float32)
    rank = jnp.dot(hits, earlier, preferred_element_type=jnp.float32)
    first = t0.astype(jnp.float32)
    second = t1.astype(jnp.float32) + 1.0
    lane = lax.broadcasted_iota(jnp.int32, (2 * CHIPS, 128), 1)
    out = jnp.zeros((2 * CHIPS, 128), jnp.float32)
    for c in range(CAP):
        chosen = jnp.where(rank == float(c), hits, 0.0)
        out = jnp.where(lane == c, jnp.sum(chosen * second, axis=1, keepdims=True), out)
        out = jnp.where(lane == CAP + c, jnp.sum(chosen * first, axis=1, keepdims=True), out)
    table[...] = out


def density_of(cand, spread, sums, lists):
    columns = jnp.transpose(cand[0:128, :], (1, 0))
    for r in range(4 * (TD + 2 * G)):
        spread[r] = jnp.broadcast_to(columns[:, r : r + 1], (128, 128))

    def one(n, carry):
        t = n // (NBD + 1)
        c = n % (NBD + 1)
        j = jnp.where(c == 0, t, lists[t, jnp.maximum(c - 1, 0)])
        xi = [cand[pl.ds(4 * t + k, 8, stride=0), :] for k in range(3)]
        total = jnp.zeros((8, 128), jnp.float32)
        for b in range(16):
            rows = slice(8 * b, 8 * b + 8)
            dx = xi[0] - spread[4 * j, rows, :]
            dy = xi[1] - spread[4 * j + 1, rows, :]
            dz = xi[2] - spread[4 * j + 2, rows, :]
            d2 = dx * dx + dy * dy + dz * dz
            total = total + jnp.exp2(spread[4 * j + 3, rows, :] - d2 * LOG2E)
        sums[t] = jnp.where(c == 0, total, sums[t] + total)
        return carry

    lax.fori_loop(0, TD * (NBD + 1), one, 0)
    return jnp.sum(sums[...], axis=1)


def density_first(pos, vel, mass, sound2, below, above, lists, table, sent, density, cand, spread, sums):
    cand[64:128, :] = jnp.zeros((64, 128), jnp.float32)
    for t in range(TD):
        span = slice(128 * t, 128 * t + 128)
        for k in range(3):
            cand[4 * t + k : 4 * t + k + 1, :] = pos[k : k + 1, span]
        cand[4 * t + 3 : 4 * t + 4, :] = jnp.log2(mass[t : t + 1, :])
    row = lax.broadcasted_iota(jnp.int32, (4 * G, 128), 0)
    for start, ref in ((4 * TD, below), (4 * TD + 4 * G, above)):
        value = ref[...]
        cand[start : start + 4 * G, :] = jnp.where(row % 4 == 3, jnp.log2(jnp.where(row % 4 == 3, value, 1.0)), value)
    rho = density_of(cand, spread, sums, lists)
    density[...] = rho
    for k in range(3):
        for t in range(TD):
            span = slice(128 * t, 128 * t + 128)
            sent[0, 8 * k + t : 8 * k + t + 1, :] = pos[k : k + 1, span]
            sent[0, 24 + 8 * k + t : 25 + 8 * k + t, :] = vel[k : k + 1, span]
    sent[0, 48:56, :] = mass[...]
    sent[0, 56:64, :] = sound2[...]
    sent[0, 64:72, :] = rho
    whole = sent[0, 0:72, :]
    for q in range(1, CHIPS):
        sent[q, 0:72, :] = whole
    for q in range(CHIPS):
        sent[q, 72:80, :] = jnp.zeros((8, 128), jnp.float32)
        sent[q, 72:74, :] = table[2 * q : 2 * q + 2, :]


def density_second(pos, mass, accel, below, above, lists, sent, density, cand, spread, sums):
    cand[64:128, :] = jnp.zeros((64, 128), jnp.float32)
    for t in range(TD):
        for k in range(3):
            cand[4 * t + k : 4 * t + k + 1, :] = pos[8 * k + t : 8 * k + t + 1, :]
        cand[4 * t + 3 : 4 * t + 4, :] = jnp.log2(mass[t : t + 1, :])
    row = lax.broadcasted_iota(jnp.int32, (4 * G, 128), 0)
    for start, ref in ((4 * TD, below), (4 * TD + 4 * G, above)):
        value = ref[...]
        cand[start : start + 4 * G, :] = jnp.where(row % 4 == 3, jnp.log2(jnp.where(row % 4 == 3, value, 1.0)), value)
    rho = density_of(cand, spread, sums, lists)
    density[...] = rho
    moved = accel[...]
    for q in range(CHIPS):
        sent[q, 0:24, :] = moved
        sent[q, 24:32, :] = rho


def pair_loop(codes, count, own, other, gains):
    for r in range(3 * TD):
        gains[r] = jnp.zeros((128, 128), jnp.float32)

    def one(n, carry):
        code = codes[n]
        base = (code // 256) * 9
        place = (code // 256) * 3
        o = code % 256
        xj, yj, zj, uj, vj, wj, sj, rj, pj, mj = [
            other[f, pl.ds(o, 8, stride=0), :] for f in range(10)
        ]
        for b in range(16):
            rows = slice(8 * b, 8 * b + 8)
            dx = own[base, rows, :] - xj
            dy = own[base + 1, rows, :] - yj
            dz = own[base + 2, rows, :] - zj
            d2 = dx * dx + dy * dy + dz * dz
            closing = (
                (own[base + 3, rows, :] - uj) * dx
                + (own[base + 4, rows, :] - vj) * dy
                + (own[base + 5, rows, :] - wj) * dz
            )
            closing = jnp.minimum(closing, 0.0)
            near = d2 + 0.01
            bottom = near * near * (own[base + 7, rows, :] + rj)
            guess = pl.reciprocal(bottom, approx=True)
            inverse = guess * (2.0 - bottom * guess)
            viscous = closing * (closing - (own[base + 6, rows, :] + sj) * near) * inverse
            strength = own[base + 8, rows, :] + pj + viscous
            weight = strength * jnp.exp2(mj - d2 * LOG2E)
            gains[place, rows, :] += weight * dx
            gains[place + 1, rows, :] += weight * dy
            gains[place + 2, rows, :] += weight * dz
        return carry

    lax.fori_loop(0, count, one, 0)
    ones = jnp.ones((8, 128), jnp.float32)
    flat = gains[...].reshape(3 * TD * 128, 128)
    return lax.dot_general(
        ones,
        flat,
        (((1,), (1,)), ((), ())),
        precision=lax.Precision.HIGHEST,
        preferred_element_type=jnp.float32,
    )


def spread_own(rows, own):
    columns = jnp.transpose(rows[0:128, :], (1, 0))
    for r in range(9 * TD):
        own[r] = jnp.broadcast_to(columns[:, r : r + 1], (128, 128))


def star_rows(x, y, z):
    radius2 = x * x + y * y + z * z + SOFT
    return -STAR / (radius2 * jnp.sqrt(radius2))


def derived(sound2, rho):
    return 0.25 * jnp.sqrt(sound2), 0.25 * rho, sound2 / rho


def fill_own(rows, fields):
    rows[72:128, :] = jnp.zeros((56, 128), jnp.float32)
    for f, value in enumerate(fields):
        for t in range(TD):
            rows[9 * t + f : 9 * t + f + 1, :] = value[t : t + 1, :]


def fill_other(other, half, fields):
    spot = slice(half * CHIPS * TD, (half + 1) * CHIPS * TD)
    for f, value in enumerate(fields):
        other[f, spot, :] = value.reshape(CHIPS * TD, 128)


def advance(summed, xs, vs):
    pull = star_rows(*xs)
    accel, speed, place = [], [], []
    for k in range(3):
        gain = jnp.concatenate(
            [summed[0:1, (3 * t + k) * 128 : (3 * t + k) * 128 + 128] for t in range(TD)], axis=0
        )
        accel.append(gain + pull * xs[k])
        speed.append(vs[k] + DT * accel[k])
        place.append(xs[k] + DT * speed[k])
    return accel, speed, place


def pairs_first(mine, twin, codes_in, ghost, pos, vel, mass, sound2, rho,
                new_pos, new_vel, accel, to_next, to_prev, codes,
                own, other, gains, rows, hits, listed, sem):
    core = lax.axis_index("core")
    for half, ref in enumerate((mine, twin)):
        got = ref[:, 72:80, :]
        named = jnp.where(core == 0, got[:, 0, :], got[:, 1, :])
        hits[half * CHIPS : (half + 1) * CHIPS, :] = named.astype(jnp.int32)
    copy = pltpu.make_async_copy(hits, listed, sem)
    copy.start()
    xs, vs = [], []
    for k in range(3):
        xs.append(jnp.concatenate([pos[k : k + 1, 128 * t : 128 * t + 128] for t in range(TD)], axis=0))
        vs.append(jnp.concatenate([vel[k : k + 1, 128 * t : 128 * t + 128] for t in range(TD)], axis=0))
    fill_own(rows, xs + vs + list(derived(sound2[...], rho[...])))
    spread_own(rows, own)
    for half, ref in enumerate((mine, twin)):
        fields = [ref[:, 8 * f : 8 * f + 8, :] for f in range(9)]
        fill_other(
            other,
            half,
            fields[0:6] + list(derived(fields[7], fields[8])) + [jnp.log2(fields[6]) + 1.0],
        )
    copy.wait()

    def plain(k, carry):
        codes[k] = codes_in[0, k]
        return carry

    lax.fori_loop(0, PAIRS, plain, 0)

    def gather(i, n):
        for c in range(CAP):
            named = listed[i, c]
            codes[n] = (named - 1) * 256 + i * TD + listed[i, CAP + c]
            n = n + jnp.where(named > 0, 1, 0)
        return n

    count = lax.fori_loop(0, 2 * CHIPS, gather, PAIRS)
    codes[255] = count
    summed = pair_loop(codes, count, own, other, gains)
    acc, speed, place = advance(summed, xs, vs)
    for k in range(3):
        accel[8 * k : 8 * k + 8, :] = acc[k]
        new_vel[8 * k : 8 * k + 8, :] = speed[k]
        new_pos[8 * k : 8 * k + 8, :] = place[k]
    for side, out in enumerate((to_next, to_prev)):
        for j in range(G):
            t = ghost[side, j]
            for k in range(3):
                out[4 * j + k : 4 * j + k + 1, :] = new_pos[pl.ds(8 * k + t, 1), :]
            out[4 * j + 3 : 4 * j + 4, :] = mass[pl.ds(t, 1), :]


def pairs_second(mine, twin, mine_new, twin_new, codes, pos, vel, sound2, rho,
                 out_pos, out_vel, out_accel, own, other, gains, rows):
    xs = [pos[8 * k : 8 * k + 8, :] for k in range(3)]
    vs = [vel[8 * k : 8 * k + 8, :] for k in range(3)]
    fill_own(rows, xs + vs + list(derived(sound2[...], rho[...])))
    spread_own(rows, own)
    for half, (ref, new) in enumerate(((mine, mine_new), (twin, twin_new))):
        old = [ref[:, 8 * f : 8 * f + 8, :] for f in range(8)]
        speed = [old[3 + k] + DT * new[:, 8 * k : 8 * k + 8, :] for k in range(3)]
        place = [old[k] + DT * speed[k] for k in range(3)]
        fill_other(
            other,
            half,
            place + speed + list(derived(old[7], new[:, 24:32, :])) + [jnp.log2(old[6]) + 1.0],
        )
    summed = pair_loop(codes, codes[255], own, other, gains)
    acc, speed, place = advance(summed, xs, vs)
    for k in range(3):
        for t in range(TD):
            span = slice(128 * t, 128 * t + 128)
            out_accel[k : k + 1, span] = acc[k][t : t + 1, :]
            out_vel[k : k + 1, span] = speed[k][t : t + 1, :]
            out_pos[k : k + 1, span] = place[k][t : t + 1, :]


def along_space(value, steps):
    count = lax.axis_size("space")
    return lax.ppermute(value, "space", [(i, (i + steps) % count) for i in range(count)])


def sector(value):
    mine = lax.all_to_all(value, "chip", 0, 0, tiled=True)
    return mine, lax.ppermute(mine, "core", [(0, 1), (1, 0)])


def local(positions, velocities, masses, sound2, ghost_list, dens_list, pair_dest, pair_tiles):
    mass = masses.reshape(TD, 128)
    snd = sound2.reshape(TD, 128)
    ghost = ghost_list.T
    dense_scratch = [
        pltpu.VMEM((136, 128), jnp.float32),
        pltpu.VMEM((4 * (TD + 2 * G), 128, 128), jnp.float32),
        pltpu.VMEM((TD, 8, 128), jnp.float32),
    ]
    pair_scratch = [
        pltpu.VMEM((9 * TD, 128, 128), jnp.float32),
        pltpu.VMEM((10, OTHERS + 8, 128), jnp.float32),
        pltpu.VMEM((3 * TD, 128, 128), jnp.float32),
        pltpu.VMEM((128, 128), jnp.float32),
    ]
    to_next, to_prev = pl.pallas_call(
        ghosts_kernel,
        out_shape=(f32(4 * G, 128), f32(4 * G, 128)),
        in_specs=[VMEM, VMEM, SMEM],
        out_specs=(VMEM, VMEM),
        name="ghosts",
    )(positions, mass, ghost)
    below = along_space(to_next, 1)
    above = along_space(to_prev, -1)
    codes_in, table = pl.pallas_call(
        routes_kernel,
        out_shape=(i32(1, PAIRS), f32(2 * CHIPS, 128)),
        in_specs=[VMEM, VMEM],
        out_specs=(VMEM, VMEM),
        name="routes",
    )(pair_dest.T, pair_tiles.T)
    sent, rho = pl.pallas_call(
        density_first,
        out_shape=(f32(CHIPS, 80, 128), f32(TD, 128)),
        in_specs=[VMEM] * 6 + [SMEM, VMEM],
        out_specs=(VMEM, VMEM),
        scratch_shapes=dense_scratch,
        name="density_first",
    )(positions, velocities, mass, snd, below, above, dens_list, table)
    mine, twin = sector(sent)
    new_pos, new_vel, accel, to_next, to_prev, codes = pl.pallas_call(
        pairs_first,
        out_shape=(
            f32(24, 128),
            f32(24, 128),
            f32(24, 128),
            f32(4 * G, 128),
            f32(4 * G, 128),
            i32(256),
        ),
        in_specs=[VMEM, VMEM, SMEM, SMEM] + [VMEM] * 5,
        out_specs=(VMEM,) * 5 + (SMEM,),
        scratch_shapes=pair_scratch
        + [
            pltpu.VMEM((2 * CHIPS, 128), jnp.int32),
            pltpu.SMEM((2 * CHIPS, 128), jnp.int32),
            pltpu.SemaphoreType.DMA,
        ],
        name="pairs_first",
    )(mine, twin, codes_in, ghost, positions, velocities, mass, snd, rho)
    below = along_space(to_next, 1)
    above = along_space(to_prev, -1)
    sent, rho = pl.pallas_call(
        density_second,
        out_shape=(f32(CHIPS, 32, 128), f32(TD, 128)),
        in_specs=[VMEM] * 5 + [SMEM],
        out_specs=(VMEM, VMEM),
        scratch_shapes=dense_scratch,
        name="density_second",
    )(new_pos, mass, accel, below, above, dens_list)
    mine_new, twin_new = sector(sent)
    out_pos, out_vel, out_accel = pl.pallas_call(
        pairs_second,
        out_shape=(f32(3, 1024), f32(3, 1024), f32(3, 1024)),
        in_specs=[VMEM] * 4 + [SMEM] + [VMEM] * 4,
        out_specs=(VMEM,) * 3,
        scratch_shapes=pair_scratch,
        name="pairs_second",
    )(mine, twin, mine_new, twin_new, codes, new_pos, new_vel, snd, rho)
    return (out_pos, out_vel, out_accel, rho.reshape(TD * 128))


def solution(mesh):
    grid = Mesh(mesh.devices.reshape(mesh.devices.shape[0], CHIPS, 2), ("space", "chip", "core"))
    every = ("space", "chip", "core")
    return jax.shard_map(
        local,
        mesh=grid,
        in_specs=(
            P(None, every),
            P(None, every),
            P(every),
            P(every),
            P(every, None),
            P(every, None),
            P(every, None),
            P(every, None),
        ),
        out_specs=(P(None, every), P(None, every), P(None, every), P(every)),
        check_vma=False,
    )
```

```python
import jax
import jax.numpy as jnp
from jax import lax
from jax.experimental import pallas as pl
from jax.experimental.pallas import tpu as pltpu
from jax.sharding import Mesh, PartitionSpec as P

TD = 8
G = 4
NBD = 6
CAP = 4
PAIRS = 64
CHIPS = 16
OTHERS = 2 * CHIPS * TD
LOG2E = 1.4426950408889634
STAR = 0.5
SOFT = 0.1
DT = 0.1
SPAN = 512
GRANT = 16 * 1024 * 1024

VMEM = pl.BlockSpec(memory_space=pltpu.VMEM)
HBM = pl.BlockSpec(memory_space=pltpu.HBM)
SMEM = pl.BlockSpec(memory_space=pltpu.SMEM)


def f32(*shape):
    return jax.ShapeDtypeStruct(shape, jnp.float32)


def i32(*shape):
    return jax.ShapeDtypeStruct(shape, jnp.int32)


def begin_kernel(pos_in, vel_in, mass_in, sound2_in, ghost_in, lists_in, dest_in, tiles_in,
                 to_next, to_prev, codes, table, pos, vel, mass, sound2, ghost_out, lists,
                 wide_pos, wide_vel, dest, tiles, ghost, sems):
    moves = (
        (ghost_in, ghost),
        (pos_in, wide_pos),
        (mass_in, mass),
        (dest_in, dest),
        (tiles_in, tiles),
        (vel_in, wide_vel),
        (sound2_in, sound2),
        (lists_in, lists),
        (ghost_in, ghost_out),
    )
    copies = [pltpu.make_async_copy(src, dst, sems.at[n]) for n, (src, dst) in enumerate(moves)]
    for copy in copies:
        copy.start()
    for copy in copies:
        copy.wait()
    for t in range(TD):
        span = slice(128 * t, 128 * t + 128)
        for k in range(3):
            pos[8 * k + t : 8 * k + t + 1, :] = wide_pos[k : k + 1, span]
            vel[8 * k + t : 8 * k + t + 1, :] = wide_vel[k : k + 1, span]
    fill_outgoing(ghost, pos, mass, to_next, to_prev)
    core = lax.axis_index("core")
    d = dest[...]
    t0 = tiles[0:1, :]
    t1 = tiles[1:2, :]
    half = (d & 1) ^ core
    code = (t0 * SPAN + half * (CHIPS * TD) + (d >> 1) * TD + t1).astype(jnp.float32)
    row = lax.broadcasted_iota(jnp.int32, (PAIRS // CAP, PAIRS), 0)
    column = lax.broadcasted_iota(jnp.int32, (PAIRS // CAP, PAIRS), 1)
    lane = lax.broadcasted_iota(jnp.int32, (PAIRS // CAP, 128), 1)
    out = jnp.zeros((PAIRS // CAP, 128), jnp.float32)
    for c in range(CAP):
        chosen = jnp.where(column == CAP * row + c, code, 0.0)
        out = jnp.where(lane == c, jnp.sum(chosen, axis=1, keepdims=True), out)
    codes[...] = out.astype(jnp.int32)
    place = lax.broadcasted_iota(jnp.int32, (2 * CHIPS, PAIRS), 0)
    hits = (place == d).astype(jnp.float32)
    earlier = (
        lax.broadcasted_iota(jnp.int32, (PAIRS, PAIRS), 0)
        < lax.broadcasted_iota(jnp.int32, (PAIRS, PAIRS), 1)
    ).astype(jnp.float32)
    rank = jnp.dot(hits, earlier, preferred_element_type=jnp.float32)
    first = t0.astype(jnp.float32)
    second = t1.astype(jnp.float32) + 1.0
    lane = lax.broadcasted_iota(jnp.int32, (2 * CHIPS, 128), 1)
    out = jnp.zeros((2 * CHIPS, 128), jnp.float32)
    for c in range(CAP):
        chosen = jnp.where(rank == float(c), hits, 0.0)
        out = jnp.where(lane == c, jnp.sum(chosen * second, axis=1, keepdims=True), out)
        out = jnp.where(lane == CAP + c, jnp.sum(chosen * first, axis=1, keepdims=True), out)
    table[...] = out


def fill_outgoing(ghost, pos, mass, to_next, to_prev):
    for side, out in enumerate((to_next, to_prev)):
        for j in range(G):
            t = ghost[side, j]
            for k in range(3):
                out[4 * j + k : 4 * j + k + 1, :] = pos[pl.ds(8 * k + t, 1), :]
            out[4 * j + 3 : 4 * j + 4, :] = mass[pl.ds(t, 1), :]


def diagonal():
    sub = lax.broadcasted_iota(jnp.int32, (8, 128), 0)
    lane = lax.broadcasted_iota(jnp.int32, (8, 128), 1)
    return [lane == 8 * b + sub for b in range(16)]


def lane_sums(blocks, picks):
    total = jnp.zeros((8, 128), jnp.float32)
    for block, pick in zip(blocks, picks):
        total = jnp.where(pick, jnp.sum(block, axis=1, keepdims=True), total)
    return jnp.sum(total, axis=0, keepdims=True)


def spread_rows(rows, first, count, out):
    columns = jnp.transpose(rows[first : first + 128, :], (1, 0))
    for r in range(count):
        out[first + r] = jnp.broadcast_to(columns[:, r : r + 1], (128, 128))


def spread_kernel(pos, vel, own, rows):
    for t in range(TD):
        for k in range(3):
            rows[6 * t + k : 6 * t + k + 1, :] = pos[8 * k + t : 8 * k + t + 1, :]
            rows[6 * t + 3 + k : 6 * t + 4 + k, :] = vel[8 * k + t : 8 * k + t + 1, :]
    rows[48:128, :] = jnp.zeros((80, 128), jnp.float32)
    spread_rows(rows, 0, 48, own)


def density_of(cand, own, rho, lists):
    picks = diagonal()

    def one(t, carry):
        listed = [t] + [lists[t, c] for c in range(NBD)]
        other = [[cand[pl.ds(4 * j + k, 8, stride=0), :] for k in range(4)] for j in listed]
        blocks = []
        for b in range(16):
            rows = slice(8 * b, 8 * b + 8)
            xi, yi, zi = [own[6 * t + k, rows, :] for k in range(3)]
            total = None
            for xj, yj, zj, mj in other:
                dx = xi - xj
                dy = yi - yj
                dz = zi - zj
                part = jnp.exp2(mj - (dx * dx + dy * dy + dz * dz) * LOG2E)
                total = part if total is None else total + part
            blocks.append(total)
        rho[pl.ds(t, 1), :] = lane_sums(blocks, picks)
        return carry

    lax.fori_loop(0, TD, one, 0)


def fill_ghosts(cand, below, above):
    row = lax.broadcasted_iota(jnp.int32, (4 * G, 128), 0)
    for start, ref in ((4 * TD, below), (4 * TD + 4 * G, above)):
        value = ref[...]
        value = jnp.where(row % 4 == 3, jnp.log2(jnp.where(row % 4 == 3, value, 1.0)), value)
        cand[start : start + 4 * G, :] = value


def fill_candidates(cand, pos, heavy, below, above):
    for t in range(TD):
        for k in range(3):
            cand[4 * t + k : 4 * t + k + 1, :] = pos[8 * k + t : 8 * k + t + 1, :]
        cand[4 * t + 3 : 4 * t + 4, :] = heavy[t : t + 1, :]
    fill_ghosts(cand, below, above)


def density_first(pos, vel, mass, sound2, below, above, lists, table, own, sent, density, cand):
    heavy = jnp.log2(mass[...])
    fill_candidates(cand, pos, heavy, below, above)
    density_of(cand, own, density, lists)
    places = pos[...]
    speeds = vel[...]
    sound = 0.25 * jnp.sqrt(sound2[...])
    rho = density[...]
    for q in range(CHIPS):
        sent[q, 0:24, :] = places
        sent[q, 24:48, :] = speeds
        sent[q, 48:56, :] = heavy + 1.0
        sent[q, 56:64, :] = sound
        sent[q, 64:72, :] = rho
        sent[q, 72:80, :] = jnp.zeros((8, 128), jnp.float32)
        sent[q, 72:74, :] = table[2 * q : 2 * q + 2, :]


def density_second(pos, mass, accel, below, above, lists, own, sent, density, cand):
    fill_candidates(cand, pos, jnp.log2(mass[...]), below, above)
    density_of(cand, own, density, lists)
    moved = accel[...]
    rho = density[...]
    for q in range(CHIPS):
        sent[q, 0:24, :] = moved
        sent[q, 24:32, :] = rho


def pair_loop(listed, own, own_state, other, gains):
    for r in range(3 * TD):
        gains[r] = jnp.zeros((128, 128), jnp.float32)

    def force(code):
        t = code >> 9
        base = t * 6
        place = t * 3
        o = code & (SPAN - 1)
        xj, yj, zj, uj, vj, wj, sj, rj, pj, mj = [
            other[f, pl.ds(o, 8, stride=0), :] for f in range(10)
        ]
        for b in range(16):
            rows = slice(8 * b, 8 * b + 8)
            dx = own[base, rows, :] - xj
            dy = own[base + 1, rows, :] - yj
            dz = own[base + 2, rows, :] - zj
            d2 = dx * dx + dy * dy + dz * dz
            closing = (
                (own[base + 3, rows, :] - uj) * dx
                + (own[base + 4, rows, :] - vj) * dy
                + (own[base + 5, rows, :] - wj) * dz
            )
            closing = jnp.minimum(closing, 0.0)
            near = d2 + 0.01
            bottom = near * near * (own_state[place + 1, rows, :] + rj)
            guess = pl.reciprocal(bottom, approx=True)
            inverse = guess * (2.0 - bottom * guess)
            viscous = closing * (closing - (own_state[place, rows, :] + sj) * near) * inverse
            strength = own_state[place + 2, rows, :] + pj + viscous
            weight = strength * jnp.exp2(mj - d2 * LOG2E)
            gains[place, rows, :] += weight * dx
            gains[place + 1, rows, :] += weight * dy
            gains[place + 2, rows, :] += weight * dz

    def one(n, carry):
        for code in [listed[n, c] for c in range(CAP)]:
            force(code)
        return carry

    lax.fori_loop(0, PAIRS // CAP + 2 * CHIPS, one, 0)


def gathered_gain(gains, gain_rows):
    picks = diagonal()
    for t in range(TD):
        for k in range(3):
            blocks = [gains[3 * t + k, 8 * b : 8 * b + 8, :] for b in range(16)]
            gain_rows[8 * k + t : 8 * k + t + 1, :] = lane_sums(blocks, picks)


def fill_own_state(rows, own_state, sound2, rho):
    state = (0.25 * jnp.sqrt(sound2), 0.25 * rho, sound2 / rho)
    rows[3 * TD : 128, :] = jnp.zeros((128 - 3 * TD, 128), jnp.float32)
    for f, value in enumerate(state):
        for t in range(TD):
            rows[3 * t + f : 3 * t + f + 1, :] = value[t : t + 1, :]
    spread_rows(rows, 0, 3 * TD, own_state)


def fill_other(other, half, fields, sound, rho, heavy):
    spot = slice(half * CHIPS * TD, (half + 1) * CHIPS * TD)
    quarter = 0.25 * rho
    for f, value in enumerate(fields + [sound, quarter, 4.0 * sound * sound / quarter, heavy]):
        other[f, spot, :] = value.reshape(CHIPS * TD, 128)


def fill_dummy(other):
    for f in range(9):
        other[f, OTHERS : OTHERS + 8, :] = jnp.zeros((8, 128), jnp.float32)
    other[9, OTHERS : OTHERS + 8, :] = jnp.full((8, 128), -1e30, jnp.float32)


def listing(codes, mine, twin, hits, listed, sem):
    core = lax.axis_index("core")
    own_rows = PAIRS // CAP
    hits[0:own_rows, :] = codes[...]
    place = lax.broadcasted_iota(jnp.int32, (CHIPS, 128), 0)
    for half, ref in enumerate((mine, twin)):
        got = ref[:, 72:80, :]
        named = jnp.where(core == 0, got[:, 0, :], got[:, 1, :])
        first = pltpu.roll(named, 128 - CAP, 1)
        code = (named.astype(jnp.int32) - 1) * SPAN + (half * CHIPS + place) * TD
        code = code + first.astype(jnp.int32)
        start = own_rows + half * CHIPS
        hits[start : start + CHIPS, :] = jnp.where(named > 0.5, code, OTHERS)
    copy = pltpu.make_async_copy(hits, listed, sem)
    copy.start()
    return copy


def advance(gain_rows, xs, vs):
    radius2 = xs[0] * xs[0] + xs[1] * xs[1] + xs[2] * xs[2] + SOFT
    pull = -STAR / (radius2 * jnp.sqrt(radius2))
    accel = [gain_rows[8 * k : 8 * k + 8, :] + pull * xs[k] for k in range(3)]
    speed = [vs[k] + DT * accel[k] for k in range(3)]
    place = [xs[k] + DT * speed[k] for k in range(3)]
    return accel, speed, place


def pairs_first(mine, twin, codes, ghost, pos, vel, mass, sound2, rho, own,
                new_pos, new_vel, accel, to_next, to_prev,
                own_state, other, gains, rows, gain_rows, hits, listed, sem):
    copy = listing(codes, mine, twin, hits, listed, sem)
    xs = [pos[8 * k : 8 * k + 8, :] for k in range(3)]
    vs = [vel[8 * k : 8 * k + 8, :] for k in range(3)]
    fill_own_state(rows, own_state, sound2[...], rho[...])
    for half, ref in enumerate((mine, twin)):
        fields = [ref[:, 8 * f : 8 * f + 8, :] for f in range(9)]
        fill_other(other, half, fields[0:6], fields[7], fields[8], fields[6])
    fill_dummy(other)
    copy.wait()
    pair_loop(listed, own, own_state, other, gains)
    gathered_gain(gains, gain_rows)
    acc, speed, place = advance(gain_rows, xs, vs)
    for k in range(3):
        accel[8 * k : 8 * k + 8, :] = acc[k]
        new_vel[8 * k : 8 * k + 8, :] = speed[k]
        new_pos[8 * k : 8 * k + 8, :] = place[k]
    fill_outgoing(ghost, new_pos, mass, to_next, to_prev)


def pairs_second(mine, twin, mine_new, twin_new, codes, pos, vel, sound2, rho, own,
                 out_pos, out_vel, out_accel, out_rho,
                 own_state, other, gains, rows, gain_rows, hits, listed, sem):
    copy = listing(codes, mine, twin, hits, listed, sem)
    out_rho[...] = rho[...]
    fill_own_state(rows, own_state, sound2[...], rho[...])
    for half, (ref, new) in enumerate(((mine, mine_new), (twin, twin_new))):
        old = [ref[:, 8 * f : 8 * f + 8, :] for f in range(8)]
        speed = [old[3 + k] + DT * new[:, 8 * k : 8 * k + 8, :] for k in range(3)]
        place = [old[k] + DT * speed[k] for k in range(3)]
        fill_other(other, half, place + speed, old[7], new[:, 24:32, :], old[6])
    fill_dummy(other)
    copy.wait()
    pair_loop(listed, own, own_state, other, gains)
    gathered_gain(gains, gain_rows)
    xs = [pos[8 * k : 8 * k + 8, :] for k in range(3)]
    vs = [vel[8 * k : 8 * k + 8, :] for k in range(3)]
    acc, speed, place = advance(gain_rows, xs, vs)
    for k in range(3):
        for t in range(TD):
            span = slice(128 * t, 128 * t + 128)
            out_accel[k : k + 1, span] = acc[k][t : t + 1, :]
            out_vel[k : k + 1, span] = speed[k][t : t + 1, :]
            out_pos[k : k + 1, span] = place[k][t : t + 1, :]


def call(kernel, outs, ins, scratch=(), name=None):
    specs = [{"s": SMEM, "v": VMEM, "h": HBM}[spec] for spec in ins]
    return pl.pallas_call(
        kernel,
        out_shape=outs,
        in_specs=specs,
        out_specs=jax.tree.map(lambda _: VMEM, outs),
        scratch_shapes=scratch,
        compiler_params=pltpu.CompilerParams(vmem_limit_bytes=GRANT),
        name=name,
    )


def along_space(value, steps):
    count = lax.axis_size("space")
    return lax.ppermute(value, "space", [(i, (i + steps) % count) for i in range(count)])


def sector(value):
    mine = lax.all_to_all(value, "chip", 0, 0, tiled=True)
    return mine, lax.ppermute(mine, "core", [(0, 1), (1, 0)])


def local(positions, velocities, masses, sound2, ghost_list, dens_list, pair_dest, pair_tiles):
    pair_scratch = [
        pltpu.VMEM((3 * TD, 128, 128), jnp.float32),
        pltpu.VMEM((10, OTHERS + 8, 128), jnp.float32),
        pltpu.VMEM((3 * TD, 128, 128), jnp.float32),
        pltpu.VMEM((128, 128), jnp.float32),
        pltpu.VMEM((3 * TD, 128), jnp.float32),
        pltpu.VMEM((PAIRS // CAP + 2 * CHIPS, 128), jnp.int32),
        pltpu.SMEM((PAIRS // CAP + 2 * CHIPS, 128), jnp.int32),
        pltpu.SemaphoreType.DMA,
    ]
    cand = [pltpu.VMEM((4 * (TD + 2 * G) + 8, 128), jnp.float32)]
    spread = [pltpu.VMEM((128, 128), jnp.float32)]
    ghost_rows = f32(4 * G, 128)
    spread_shape = f32(6 * TD, 128, 128)
    to_next, to_prev, codes, table, pos, vel, mass, snd, ghost, lists = call(
        begin_kernel,
        (
            ghost_rows,
            ghost_rows,
            i32(PAIRS // CAP, 128),
            f32(2 * CHIPS, 128),
            f32(24, 128),
            f32(24, 128),
            f32(TD, 128),
            f32(TD, 128),
            i32(2, G),
            i32(TD, NBD),
        ),
        "hhhhhhhh",
        scratch=[
            pltpu.VMEM((3, 128 * TD), jnp.float32),
            pltpu.VMEM((3, 128 * TD), jnp.float32),
            pltpu.VMEM((1, PAIRS), jnp.int32),
            pltpu.VMEM((2, PAIRS), jnp.int32),
            pltpu.SMEM((2, G), jnp.int32),
            pltpu.SemaphoreType.DMA((9,)),
        ],
        name="begin",
    )(
        *(
            pltpu.with_memory_space_constraint(value, pltpu.HBM)
            for value in (
                positions,
                velocities,
                masses.reshape(TD, 128),
                sound2.reshape(TD, 128),
                ghost_list.T,
                dens_list,
                pair_dest.T,
                pair_tiles.T,
            )
        )
    )
    below = along_space(to_next, 1)
    above = along_space(to_prev, -1)
    own = call(spread_kernel, spread_shape, "vv", scratch=spread, name="spread_first")(pos, vel)
    sent, rho = call(
        density_first,
        (f32(CHIPS, 80, 128), f32(TD, 128)),
        "vvvvvvsvv",
        scratch=cand,
        name="density_first",
    )(pos, vel, mass, snd, below, above, lists, table, own)
    mine, twin = sector(sent)
    new_pos, new_vel, accel, to_next, to_prev = call(
        pairs_first,
        (f32(24, 128), f32(24, 128), f32(24, 128), ghost_rows, ghost_rows),
        "vvvsvvvvvv",
        scratch=pair_scratch,
        name="pairs_first",
    )(mine, twin, codes, ghost, pos, vel, mass, snd, rho, own)
    below = along_space(to_next, 1)
    above = along_space(to_prev, -1)
    own = call(spread_kernel, spread_shape, "vv", scratch=spread, name="spread_second")(
        new_pos, new_vel
    )
    sent, rho = call(
        density_second,
        (f32(CHIPS, 32, 128), f32(TD, 128)),
        "vvvvvsv",
        scratch=cand,
        name="density_second",
    )(new_pos, mass, accel, below, above, lists, own)
    mine_new, twin_new = sector(sent)
    out_pos, out_vel, out_accel, out_rho = call(
        pairs_second,
        (f32(3, 1024), f32(3, 1024), f32(3, 1024), f32(TD, 128)),
        "vvvvvvvvvv",
        scratch=pair_scratch,
        name="pairs_second",
    )(mine, twin, mine_new, twin_new, codes, new_pos, new_vel, snd, rho, own)
    return (out_pos, out_vel, out_accel, out_rho.reshape(TD * 128))


def solution(mesh):
    grid = Mesh(mesh.devices.reshape(mesh.devices.shape[0], CHIPS, 2), ("space", "chip", "core"))
    every = ("space", "chip", "core")
    return jax.shard_map(
        local,
        mesh=grid,
        in_specs=(
            P(None, every),
            P(None, every),
            P(every),
            P(every),
            P(every, None),
            P(every, None),
            P(every, None),
            P(every, None),
        ),
        out_specs=(P(None, every), P(None, every), P(None, every), P(every)),
        check_vma=False,
    )
```

```python
import math

import jax
import jax.numpy as jnp
from jax import lax
from jax.experimental import pallas as pl
from jax.experimental.pallas import tpu as pltpu
from jax.sharding import Mesh, PartitionSpec as P

TD = 8
G = 4
NBD = 6
CAP = 4
PAIRS = 64
CHIPS = 16
OTHERS = 2 * CHIPS * TD
LOG2E = 1.4426950408889634
ROOT = LOG2E**0.5
STAR = 0.5
SOFT = 0.1
DT = 0.1
SPAN = 512
UNROLL = 8
GRANT = 16 * 1024 * 1024

VMEM = pl.BlockSpec(memory_space=pltpu.VMEM)
HBM = pl.BlockSpec(memory_space=pltpu.HBM)
SMEM = pl.BlockSpec(memory_space=pltpu.SMEM)


def f32(*shape):
    return jax.ShapeDtypeStruct(shape, jnp.float32)


def i32(*shape):
    return jax.ShapeDtypeStruct(shape, jnp.int32)


def begin_kernel(pos_in, vel_in, mass_in, sound2_in, ghost_in, lists_in, dest_in, tiles_in,
                 to_next, to_prev, codes, table, pos, vel, mass, sound2, ghost_out, lists,
                 wide_pos, wide_vel, dest, tiles, ghost, sems):
    moves = (
        (ghost_in, ghost),
        (pos_in, wide_pos),
        (mass_in, mass),
        (dest_in, dest),
        (tiles_in, tiles),
        (vel_in, wide_vel),
        (sound2_in, sound2),
        (lists_in, lists),
        (ghost_in, ghost_out),
    )
    copies = [pltpu.make_async_copy(src, dst, sems.at[n]) for n, (src, dst) in enumerate(moves)]
    for copy in copies:
        copy.start()
    for copy in copies:
        copy.wait()
    for t in range(TD):
        span = slice(128 * t, 128 * t + 128)
        for k in range(3):
            pos[8 * k + t : 8 * k + t + 1, :] = wide_pos[k : k + 1, span]
            vel[8 * k + t : 8 * k + t + 1, :] = wide_vel[k : k + 1, span]
    fill_outgoing(ghost, pos, mass, to_next, to_prev)
    core = lax.axis_index("core")
    d = dest[...]
    t0 = tiles[0:1, :]
    t1 = tiles[1:2, :]
    half = (d & 1) ^ core
    code = (t0 * SPAN + half * (CHIPS * TD) + (d >> 1) * TD + t1).astype(jnp.float32)
    row = lax.broadcasted_iota(jnp.int32, (PAIRS // CAP, PAIRS), 0)
    column = lax.broadcasted_iota(jnp.int32, (PAIRS // CAP, PAIRS), 1)
    lane = lax.broadcasted_iota(jnp.int32, (PAIRS // CAP, 128), 1)
    out = jnp.zeros((PAIRS // CAP, 128), jnp.float32)
    for c in range(CAP):
        chosen = jnp.where(column == CAP * row + c, code, 0.0)
        out = jnp.where(lane == c, jnp.sum(chosen, axis=1, keepdims=True), out)
    codes[...] = out.astype(jnp.int32)
    place = lax.broadcasted_iota(jnp.int32, (2 * CHIPS, PAIRS), 0)
    hits = (place == d).astype(jnp.float32)
    earlier = (
        lax.broadcasted_iota(jnp.int32, (PAIRS, PAIRS), 0)
        < lax.broadcasted_iota(jnp.int32, (PAIRS, PAIRS), 1)
    ).astype(jnp.float32)
    rank = jnp.dot(hits, earlier, preferred_element_type=jnp.float32)
    first = t0.astype(jnp.float32)
    second = t1.astype(jnp.float32) + 1.0
    lane = lax.broadcasted_iota(jnp.int32, (2 * CHIPS, 128), 1)
    out = jnp.zeros((2 * CHIPS, 128), jnp.float32)
    for c in range(CAP):
        chosen = jnp.where(rank == float(c), hits, 0.0)
        out = jnp.where(lane == c, jnp.sum(chosen * second, axis=1, keepdims=True), out)
        out = jnp.where(lane == CAP + c, jnp.sum(chosen * first, axis=1, keepdims=True), out)
    table[...] = out


def fill_outgoing(ghost, pos, mass, to_next, to_prev):
    for side, out in enumerate((to_next, to_prev)):
        for j in range(G):
            t = ghost[side, j]
            for k in range(3):
                out[4 * j + k : 4 * j + k + 1, :] = pos[pl.ds(8 * k + t, 1), :]
            out[4 * j + 3 : 4 * j + 4, :] = mass[pl.ds(t, 1), :]


def diagonal():
    sub = lax.broadcasted_iota(jnp.int32, (8, 128), 0)
    lane = lax.broadcasted_iota(jnp.int32, (8, 128), 1)
    return [lane == 8 * b + sub for b in range(16)]


def lane_sums(blocks, picks):
    total = jnp.zeros((8, 128), jnp.float32)
    for block, pick in zip(blocks, picks):
        total = jnp.where(pick, jnp.sum(block, axis=1, keepdims=True), total)
    return jnp.sum(total, axis=0, keepdims=True)


def spread_places(pos, own, rows):
    spread_tiles([pos[8 * k : 8 * k + 8, :] * ROOT for k in range(3)], own, rows)


def spread_rest(vel, sound2, rho, own, rows):
    fields = [vel[8 * k : 8 * k + 8, :] for k in range(3)]
    square = sound2[...]
    dense = rho[...]
    fields += [0.25 / ROOT * jnp.sqrt(square), 0.25 / LOG2E * dense, square / dense]
    spread_tiles(fields, own, rows)


def spread_tiles(fields, own, rows):
    count = len(fields)
    for f, value in enumerate(fields):
        for t in range(TD):
            rows[count * t + f : count * t + f + 1, :] = value[t : t + 1, :]
    rows[count * TD : 128, :] = jnp.zeros((128 - count * TD, 128), jnp.float32)
    columns = jnp.transpose(rows[...], (1, 0))
    for r in range(count * TD):
        own[r] = jnp.broadcast_to(columns[:, r : r + 1], (128, 128))


def density_of(cand, own, rho, lists):
    picks = diagonal()

    def one(t, carry):
        listed = [t] + [lists[t, c] for c in range(NBD)]
        other = [[cand[pl.ds(4 * j + k, 8, stride=0), :] for k in range(4)] for j in listed]
        blocks = []
        for b in range(16):
            rows = slice(8 * b, 8 * b + 8)
            xi, yi, zi = [own[3 * t + k, rows, :] for k in range(3)]
            total = None
            for xj, yj, zj, mj in other:
                dx = xi - xj
                dy = yi - yj
                dz = zi - zj
                part = jnp.exp2(mj - (dx * dx + dy * dy + dz * dz))
                total = part if total is None else total + part
            blocks.append(total)
        rho[pl.ds(t, 1), :] = lane_sums(blocks, picks)
        return carry

    lax.fori_loop(0, TD, one, 0)


def fill_ghosts(cand, below, above):
    row = lax.broadcasted_iota(jnp.int32, (4 * G, 128), 0)
    for start, ref in ((4 * TD, below), (4 * TD + 4 * G, above)):
        value = ref[...]
        value = jnp.where(row % 4 == 3, jnp.log2(jnp.where(row % 4 == 3, value, 1.0)), value * ROOT)
        cand[start : start + 4 * G, :] = value


def fill_candidates(cand, pos, heavy, below, above):
    for t in range(TD):
        for k in range(3):
            cand[4 * t + k : 4 * t + k + 1, :] = pos[8 * k + t : 8 * k + t + 1, :] * ROOT
        cand[4 * t + 3 : 4 * t + 4, :] = heavy[t : t + 1, :]
    fill_ghosts(cand, below, above)


def density_first(pos, vel, mass, sound2, below, above, lists, table, own, sent, density, cand):
    heavy = jnp.log2(mass[...])
    fill_candidates(cand, pos, heavy, below, above)
    density_of(cand, own, density, lists)
    places = pos[...]
    speeds = vel[...]
    sound = 0.25 / ROOT * jnp.sqrt(sound2[...])
    rho = density[...]
    for q in range(CHIPS):
        sent[q, 0:24, :] = places
        sent[q, 24:48, :] = speeds
        sent[q, 48:56, :] = heavy + (1.0 - math.log2(ROOT))
        sent[q, 56:64, :] = sound
        sent[q, 64:72, :] = rho
        sent[q, 72:80, :] = jnp.zeros((8, 128), jnp.float32)
        sent[q, 72:74, :] = table[2 * q : 2 * q + 2, :]


def density_second(pos, mass, accel, below, above, lists, own, sent, density, cand):
    fill_candidates(cand, pos, jnp.log2(mass[...]), below, above)
    density_of(cand, own, density, lists)
    moved = accel[...]
    rho = density[...]
    for q in range(CHIPS):
        sent[q, 0:24, :] = moved
        sent[q, 24:32, :] = rho


def pair_loop(listed, own, own_rest, other, gains):
    for r in range(3 * TD):
        gains[r] = jnp.zeros((128, 128), jnp.float32)

    def force(code):
        t = code >> 9
        place = t * 3
        rest = t * 6
        o = code & (SPAN - 1)
        xj, yj, zj, uj, vj, wj, sj, rj, pj, mj = [
            other[f, pl.ds(o, 8, stride=0), :] for f in range(10)
        ]
        for b in range(16):
            rows = slice(8 * b, 8 * b + 8)
            dx = own[place, rows, :] - xj
            dy = own[place + 1, rows, :] - yj
            dz = own[place + 2, rows, :] - zj
            d2 = dx * dx + dy * dy + dz * dz
            closing = (
                (own_rest[rest, rows, :] - uj) * dx
                + (own_rest[rest + 1, rows, :] - vj) * dy
                + (own_rest[rest + 2, rows, :] - wj) * dz
            )
            closing = jnp.minimum(closing, 0.0)
            near = d2 + 0.01 * LOG2E
            bottom = near * near * (own_rest[rest + 4, rows, :] + rj)
            viscous = closing * (closing - (own_rest[rest + 3, rows, :] + sj) * near) / bottom
            strength = own_rest[rest + 5, rows, :] + pj + viscous
            weight = strength * jnp.exp2(mj - d2)
            gains[place, rows, :] += weight * dx
            gains[place + 1, rows, :] += weight * dy
            gains[place + 2, rows, :] += weight * dz

    def one(n, carry):
        for u in range(UNROLL):
            force(listed[(UNROLL // CAP) * n + u // CAP, u % CAP])
        return carry

    lax.fori_loop(0, (PAIRS + 2 * CHIPS * CAP) // UNROLL, one, 0)


def gathered_gain(gains, gain_rows):
    picks = diagonal()
    for t in range(TD):
        for k in range(3):
            blocks = [gains[3 * t + k, 8 * b : 8 * b + 8, :] for b in range(16)]
            gain_rows[8 * k + t : 8 * k + t + 1, :] = lane_sums(blocks, picks)


def fill_other(other, half, fields, sound, rho, heavy):
    spot = slice(half * CHIPS * TD, (half + 1) * CHIPS * TD)
    pressure = 16.0 * LOG2E * sound * sound / rho
    fields = [ROOT * x for x in fields[0:3]] + list(fields[3:6])
    for f, value in enumerate(fields + [sound, 0.25 / LOG2E * rho, pressure, heavy]):
        other[f, spot, :] = value.reshape(CHIPS * TD, 128)


def fill_dummy(other):
    for f in range(9):
        other[f, OTHERS : OTHERS + 8, :] = jnp.zeros((8, 128), jnp.float32)
    other[9, OTHERS : OTHERS + 8, :] = jnp.full((8, 128), -1e30, jnp.float32)


def listing(codes, mine, twin, hits, listed, sem):
    core = lax.axis_index("core")
    own_rows = PAIRS // CAP
    hits[0:own_rows, :] = codes[...]
    place = lax.broadcasted_iota(jnp.int32, (CHIPS, 128), 0)
    for half, ref in enumerate((mine, twin)):
        got = ref[:, 72:80, :]
        named = jnp.where(core == 0, got[:, 0, :], got[:, 1, :])
        first = pltpu.roll(named, 128 - CAP, 1)
        code = (named.astype(jnp.int32) - 1) * SPAN + (half * CHIPS + place) * TD
        code = code + first.astype(jnp.int32)
        start = own_rows + half * CHIPS
        hits[start : start + CHIPS, :] = jnp.where(named > 0.5, code, OTHERS)
    copy = pltpu.make_async_copy(hits, listed, sem)
    copy.start()
    return copy


def advance(gain_rows, xs, vs):
    radius2 = xs[0] * xs[0] + xs[1] * xs[1] + xs[2] * xs[2] + SOFT
    pull = -STAR / (radius2 * jnp.sqrt(radius2))
    accel = [gain_rows[8 * k : 8 * k + 8, :] + pull * xs[k] for k in range(3)]
    speed = [vs[k] + DT * accel[k] for k in range(3)]
    place = [xs[k] + DT * speed[k] for k in range(3)]
    return accel, speed, place


def pairs_first(mine, twin, codes, ghost, pos, vel, mass, own, own_rest,
                new_pos, new_vel, accel, to_next, to_prev,
                other, gains, gain_rows, hits, listed, sem):
    copy = listing(codes, mine, twin, hits, listed, sem)
    xs = [pos[8 * k : 8 * k + 8, :] for k in range(3)]
    vs = [vel[8 * k : 8 * k + 8, :] for k in range(3)]
    for half, ref in enumerate((mine, twin)):
        fields = [ref[:, 8 * f : 8 * f + 8, :] for f in range(9)]
        fill_other(other, half, fields[0:6], fields[7], fields[8], fields[6])
    fill_dummy(other)
    copy.wait()
    pair_loop(listed, own, own_rest, other, gains)
    gathered_gain(gains, gain_rows)
    acc, speed, place = advance(gain_rows, xs, vs)
    for k in range(3):
        accel[8 * k : 8 * k + 8, :] = acc[k]
        new_vel[8 * k : 8 * k + 8, :] = speed[k]
        new_pos[8 * k : 8 * k + 8, :] = place[k]
    fill_outgoing(ghost, new_pos, mass, to_next, to_prev)


def pairs_second(mine, twin, mine_new, twin_new, codes, pos, vel, rho, own, own_rest,
                 out_pos, out_vel, out_accel, out_rho,
                 other, gains, gain_rows, hits, listed, sem):
    copy = listing(codes, mine, twin, hits, listed, sem)
    out_rho[...] = rho[...]
    for half, (ref, new) in enumerate(((mine, mine_new), (twin, twin_new))):
        old = [ref[:, 8 * f : 8 * f + 8, :] for f in range(8)]
        speed = [old[3 + k] + DT * new[:, 8 * k : 8 * k + 8, :] for k in range(3)]
        place = [old[k] + DT * speed[k] for k in range(3)]
        fill_other(other, half, place + speed, old[7], new[:, 24:32, :], old[6])
    fill_dummy(other)
    copy.wait()
    pair_loop(listed, own, own_rest, other, gains)
    gathered_gain(gains, gain_rows)
    xs = [pos[8 * k : 8 * k + 8, :] for k in range(3)]
    vs = [vel[8 * k : 8 * k + 8, :] for k in range(3)]
    acc, speed, place = advance(gain_rows, xs, vs)
    for k in range(3):
        for t in range(TD):
            span = slice(128 * t, 128 * t + 128)
            out_accel[k : k + 1, span] = acc[k][t : t + 1, :]
            out_vel[k : k + 1, span] = speed[k][t : t + 1, :]
            out_pos[k : k + 1, span] = place[k][t : t + 1, :]


def call(kernel, outs, ins, scratch=(), name=None):
    specs = [{"s": SMEM, "v": VMEM, "h": HBM}[spec] for spec in ins]
    return pl.pallas_call(
        kernel,
        out_shape=outs,
        in_specs=specs,
        out_specs=jax.tree.map(lambda _: VMEM, outs),
        scratch_shapes=scratch,
        compiler_params=pltpu.CompilerParams(vmem_limit_bytes=GRANT),
        name=name,
    )


def along_space(value, steps):
    count = lax.axis_size("space")
    return lax.ppermute(value, "space", [(i, (i + steps) % count) for i in range(count)])


def sector(value):
    mine = lax.all_to_all(value, "chip", 0, 0, tiled=True)
    return mine, lax.ppermute(mine, "core", [(0, 1), (1, 0)])


def local(positions, velocities, masses, sound2, ghost_list, dens_list, pair_dest, pair_tiles):
    pair_scratch = [
        pltpu.VMEM((10, OTHERS + 8, 128), jnp.float32),
        pltpu.VMEM((3 * TD, 128, 128), jnp.float32),
        pltpu.VMEM((3 * TD, 128), jnp.float32),
        pltpu.VMEM((PAIRS // CAP + 2 * CHIPS, 128), jnp.int32),
        pltpu.SMEM((PAIRS // CAP + 2 * CHIPS, 128), jnp.int32),
        pltpu.SemaphoreType.DMA,
    ]
    cand = [pltpu.VMEM((4 * (TD + 2 * G) + 8, 128), jnp.float32)]
    spread = [pltpu.VMEM((128, 128), jnp.float32)]
    ghost_rows = f32(4 * G, 128)
    places_shape = f32(3 * TD, 128, 128)
    rest_shape = f32(6 * TD, 128, 128)
    to_next, to_prev, codes, table, pos, vel, mass, snd, ghost, lists = call(
        begin_kernel,
        (
            ghost_rows,
            ghost_rows,
            i32(PAIRS // CAP, 128),
            f32(2 * CHIPS, 128),
            f32(24, 128),
            f32(24, 128),
            f32(TD, 128),
            f32(TD, 128),
            i32(2, G),
            i32(TD, NBD),
        ),
        "hhhhhhhh",
        scratch=[
            pltpu.VMEM((3, 128 * TD), jnp.float32),
            pltpu.VMEM((3, 128 * TD), jnp.float32),
            pltpu.VMEM((1, PAIRS), jnp.int32),
            pltpu.VMEM((2, PAIRS), jnp.int32),
            pltpu.SMEM((2, G), jnp.int32),
            pltpu.SemaphoreType.DMA((9,)),
        ],
        name="begin",
    )(
        *(
            pltpu.with_memory_space_constraint(value, pltpu.HBM)
            for value in (
                positions,
                velocities,
                masses.reshape(TD, 128),
                sound2.reshape(TD, 128),
                ghost_list.T,
                dens_list,
                pair_dest.T,
                pair_tiles.T,
            )
        )
    )
    below = along_space(to_next, 1)
    above = along_space(to_prev, -1)
    own = call(spread_places, places_shape, "v", scratch=spread, name="places_first")(pos)
    sent, rho = call(
        density_first,
        (f32(CHIPS, 80, 128), f32(TD, 128)),
        "vvvvvvsvv",
        scratch=cand,
        name="density_first",
    )(pos, vel, mass, snd, below, above, lists, table, own)
    mine, twin = sector(sent)
    rest = call(spread_rest, rest_shape, "vvv", scratch=spread, name="rest_first")(vel, snd, rho)
    new_pos, new_vel, accel, to_next, to_prev = call(
        pairs_first,
        (f32(24, 128), f32(24, 128), f32(24, 128), ghost_rows, ghost_rows),
        "vvvsvvvvv",
        scratch=pair_scratch,
        name="pairs_first",
    )(mine, twin, codes, ghost, pos, vel, mass, own, rest)
    below = along_space(to_next, 1)
    above = along_space(to_prev, -1)
    own = call(spread_places, places_shape, "v", scratch=spread, name="places_second")(new_pos)
    sent, rho = call(
        density_second,
        (f32(CHIPS, 32, 128), f32(TD, 128)),
        "vvvvvsv",
        scratch=cand,
        name="density_second",
    )(new_pos, mass, accel, below, above, lists, own)
    mine_new, twin_new = sector(sent)
    rest = call(spread_rest, rest_shape, "vvv", scratch=spread, name="rest_second")(
        new_vel, snd, rho
    )
    out_pos, out_vel, out_accel, out_rho = call(
        pairs_second,
        (f32(3, 1024), f32(3, 1024), f32(3, 1024), f32(TD, 128)),
        "vvvvvvvvvv",
        scratch=pair_scratch,
        name="pairs_second",
    )(mine, twin, mine_new, twin_new, codes, new_pos, new_vel, rho, own, rest)
    return (out_pos, out_vel, out_accel, out_rho.reshape(TD * 128))


def solution(mesh):
    grid = Mesh(mesh.devices.reshape(mesh.devices.shape[0], CHIPS, 2), ("space", "chip", "core"))
    every = ("space", "chip", "core")
    return jax.shard_map(
        local,
        mesh=grid,
        in_specs=(
            P(None, every),
            P(None, every),
            P(every),
            P(every),
            P(every, None),
            P(every, None),
            P(every, None),
            P(every, None),
        ),
        out_specs=(P(None, every), P(None, every), P(None, every), P(every)),
        check_vma=False,
    )
```

```python
import math

import jax
import jax.numpy as jnp
from jax import lax
from jax.experimental import pallas as pl
from jax.experimental.pallas import tpu as pltpu
from jax.sharding import Mesh, PartitionSpec as P

TD = 8
G = 4
NBD = 6
CAP = 4
PAIRS = 64
CHIPS = 16
OTHERS = 2 * CHIPS * TD
LOG2E = 1.4426950408889634
ROOT = LOG2E**0.5
STAR = 0.5
SOFT = 0.1
DT = 0.1
SPAN = 512
UNROLL = 16
GRANT = 16 * 1024 * 1024

VMEM = pl.BlockSpec(memory_space=pltpu.VMEM)
HBM = pl.BlockSpec(memory_space=pltpu.HBM)
SMEM = pl.BlockSpec(memory_space=pltpu.SMEM)


def f32(*shape):
    return jax.ShapeDtypeStruct(shape, jnp.float32)


def i32(*shape):
    return jax.ShapeDtypeStruct(shape, jnp.int32)


def begin_kernel(pos_in, vel_in, mass_in, sound2_in, ghost_in, lists_in, dest_in, tiles_in,
                 to_next, to_prev, codes, table, pos, vel, mass, sound2, ghost_out, lists,
                 wide_pos, wide_vel, dest, tiles, ghost, sems):
    moves = (
        (ghost_in, ghost),
        (pos_in, wide_pos),
        (mass_in, mass),
        (dest_in, dest),
        (tiles_in, tiles),
        (vel_in, wide_vel),
        (sound2_in, sound2),
        (lists_in, lists),
        (ghost_in, ghost_out),
    )
    copies = [pltpu.make_async_copy(src, dst, sems.at[n]) for n, (src, dst) in enumerate(moves)]
    for copy in copies:
        copy.start()
    for copy in copies:
        copy.wait()
    for t in range(TD):
        span = slice(128 * t, 128 * t + 128)
        for k in range(3):
            pos[8 * k + t : 8 * k + t + 1, :] = wide_pos[k : k + 1, span]
            vel[8 * k + t : 8 * k + t + 1, :] = wide_vel[k : k + 1, span]
    fill_outgoing(ghost, pos, mass, to_next, to_prev)
    core = lax.axis_index("core")
    d = dest[...]
    t0 = tiles[0:1, :]
    t1 = tiles[1:2, :]
    half = (d & 1) ^ core
    code = (t0 * SPAN + half * (CHIPS * TD) + (d >> 1) * TD + t1).astype(jnp.float32)
    row = lax.broadcasted_iota(jnp.int32, (PAIRS // CAP, PAIRS), 0)
    column = lax.broadcasted_iota(jnp.int32, (PAIRS // CAP, PAIRS), 1)
    lane = lax.broadcasted_iota(jnp.int32, (PAIRS // CAP, 128), 1)
    out = jnp.zeros((PAIRS // CAP, 128), jnp.float32)
    for c in range(CAP):
        chosen = jnp.where(column == CAP * row + c, code, 0.0)
        out = jnp.where(lane == c, jnp.sum(chosen, axis=1, keepdims=True), out)
    codes[...] = out.astype(jnp.int32)
    place = lax.broadcasted_iota(jnp.int32, (2 * CHIPS, PAIRS), 0)
    hits = (place == d).astype(jnp.float32)
    earlier = (
        lax.broadcasted_iota(jnp.int32, (PAIRS, PAIRS), 0)
        < lax.broadcasted_iota(jnp.int32, (PAIRS, PAIRS), 1)
    ).astype(jnp.float32)
    rank = jnp.dot(hits, earlier, preferred_element_type=jnp.float32)
    first = t0.astype(jnp.float32)
    second = t1.astype(jnp.float32) + 1.0
    lane = lax.broadcasted_iota(jnp.int32, (2 * CHIPS, 128), 1)
    out = jnp.zeros((2 * CHIPS, 128), jnp.float32)
    for c in range(CAP):
        chosen = jnp.where(rank == float(c), hits, 0.0)
        out = jnp.where(lane == c, jnp.sum(chosen * second, axis=1, keepdims=True), out)
        out = jnp.where(lane == CAP + c, jnp.sum(chosen * first, axis=1, keepdims=True), out)
    table[...] = out


def fill_outgoing(ghost, pos, mass, to_next, to_prev):
    for side, out in enumerate((to_next, to_prev)):
        for j in range(G):
            t = ghost[side, j]
            for k in range(3):
                out[4 * j + k : 4 * j + k + 1, :] = pos[pl.ds(8 * k + t, 1), :]
            out[4 * j + 3 : 4 * j + 4, :] = mass[pl.ds(t, 1), :]


def diagonal():
    sub = lax.broadcasted_iota(jnp.int32, (8, 128), 0)
    lane = lax.broadcasted_iota(jnp.int32, (8, 128), 1)
    return [lane == 8 * b + sub for b in range(16)]


def lane_sums(blocks, picks):
    total = jnp.zeros((8, 128), jnp.float32)
    for block, pick in zip(blocks, picks):
        total = jnp.where(pick, jnp.sum(block, axis=1, keepdims=True), total)
    return jnp.sum(total, axis=0, keepdims=True)


def spread_places(pos, own, rows):
    spread_tiles([pos[8 * k : 8 * k + 8, :] * ROOT for k in range(3)], own, rows)


def spread_rest(vel, sound2, rho, own, rows):
    fields = [vel[8 * k : 8 * k + 8, :] for k in range(3)]
    square = sound2[...]
    dense = rho[...]
    fields += [0.25 / ROOT * jnp.sqrt(square), 0.25 / LOG2E * dense, square / dense]
    spread_tiles(fields, own, rows)


def spread_tiles(fields, own, rows):
    count = len(fields)
    for f, value in enumerate(fields):
        for t in range(TD):
            rows[count * t + f : count * t + f + 1, :] = value[t : t + 1, :]
    rows[count * TD : 128, :] = jnp.zeros((128 - count * TD, 128), jnp.float32)
    columns = jnp.transpose(rows[...], (1, 0))
    for r in range(count * TD):
        own[r] = jnp.broadcast_to(columns[:, r : r + 1], (128, 128))


def density_of(cand, own, rho, lists):
    picks = diagonal()

    def tile(t):
        listed = [t] + [lists[t, c] for c in range(NBD)]
        other = [[cand[pl.ds(4 * j + k, 8, stride=0), :] for k in range(4)] for j in listed]
        blocks = []
        for b in range(16):
            rows = slice(8 * b, 8 * b + 8)
            xi, yi, zi = [own[3 * t + k, rows, :] for k in range(3)]
            total = None
            for xj, yj, zj, mj in other:
                dx = xi - xj
                dy = yi - yj
                dz = zi - zj
                part = jnp.exp2(mj - (dx * dx + dy * dy + dz * dz))
                total = part if total is None else total + part
            blocks.append(total)
        rho[pl.ds(t, 1), :] = lane_sums(blocks, picks)

    def one(n, carry):
        for u in range(2):
            tile(2 * n + u)
        return carry

    lax.fori_loop(0, TD // 2, one, 0)


def fill_ghosts(cand, below, above):
    row = lax.broadcasted_iota(jnp.int32, (4 * G, 128), 0)
    for start, ref in ((4 * TD, below), (4 * TD + 4 * G, above)):
        value = ref[...]
        value = jnp.where(row % 4 == 3, jnp.log2(jnp.where(row % 4 == 3, value, 1.0)), value * ROOT)
        cand[start : start + 4 * G, :] = value


def fill_candidates(cand, pos, heavy, below, above):
    for t in range(TD):
        for k in range(3):
            cand[4 * t + k : 4 * t + k + 1, :] = pos[8 * k + t : 8 * k + t + 1, :] * ROOT
        cand[4 * t + 3 : 4 * t + 4, :] = heavy[t : t + 1, :]
    fill_ghosts(cand, below, above)


def density_first(pos, vel, mass, sound2, below, above, lists, table, own, sent, density, cand):
    heavy = jnp.log2(mass[...])
    fill_candidates(cand, pos, heavy, below, above)
    density_of(cand, own, density, lists)
    places = pos[...]
    speeds = vel[...]
    sound = 0.25 / ROOT * jnp.sqrt(sound2[...])
    rho = density[...]
    for q in range(CHIPS):
        sent[q, 0:24, :] = places
        sent[q, 24:48, :] = speeds
        sent[q, 48:56, :] = heavy + (1.0 - math.log2(ROOT))
        sent[q, 56:64, :] = sound
        sent[q, 64:72, :] = rho
        sent[q, 72:80, :] = jnp.zeros((8, 128), jnp.float32)
        sent[q, 72:74, :] = table[2 * q : 2 * q + 2, :]


def density_second(pos, mass, accel, below, above, lists, own, sent, density, cand):
    fill_candidates(cand, pos, jnp.log2(mass[...]), below, above)
    density_of(cand, own, density, lists)
    moved = accel[...]
    rho = density[...]
    for q in range(CHIPS):
        sent[q, 0:24, :] = moved
        sent[q, 24:32, :] = rho


def pair_loop(listed, own, own_rest, other, gains):
    for r in range(3 * TD):
        gains[r] = jnp.zeros((128, 128), jnp.float32)

    def force(code):
        t = code >> 9
        place = t * 3
        rest = t * 6
        o = code & (SPAN - 1)
        xj, yj, zj, uj, vj, wj, sj, rj, pj, mj = [
            other[f, pl.ds(o, 8, stride=0), :] for f in range(10)
        ]
        for b in range(16):
            rows = slice(8 * b, 8 * b + 8)
            dx = own[place, rows, :] - xj
            dy = own[place + 1, rows, :] - yj
            dz = own[place + 2, rows, :] - zj
            d2 = dx * dx + dy * dy + dz * dz
            closing = (
                (own_rest[rest, rows, :] - uj) * dx
                + (own_rest[rest + 1, rows, :] - vj) * dy
                + (own_rest[rest + 2, rows, :] - wj) * dz
            )
            near = d2 + 0.01 * LOG2E
            closing = jnp.minimum(closing, 0.0) / near
            sound = own_rest[rest + 3, rows, :] + sj
            viscous = closing * (closing - sound) / (own_rest[rest + 4, rows, :] + rj)
            strength = own_rest[rest + 5, rows, :] + pj + viscous
            weight = strength * jnp.exp2(mj - d2)
            gains[place, rows, :] += weight * dx
            gains[place + 1, rows, :] += weight * dy
            gains[place + 2, rows, :] += weight * dz

    def one(n, carry):
        for u in range(UNROLL):
            force(listed[(UNROLL // CAP) * n + u // CAP, u % CAP])
        return carry

    lax.fori_loop(0, (PAIRS + 2 * CHIPS * CAP) // UNROLL, one, 0)


def gathered_gain(gains, gain_rows):
    picks = diagonal()
    for t in range(TD):
        for k in range(3):
            blocks = [gains[3 * t + k, 8 * b : 8 * b + 8, :] for b in range(16)]
            gain_rows[8 * k + t : 8 * k + t + 1, :] = lane_sums(blocks, picks)


def fill_other(other, half, fields, sound, rho, heavy):
    spot = slice(half * CHIPS * TD, (half + 1) * CHIPS * TD)
    pressure = 16.0 * LOG2E * sound * sound / rho
    fields = [ROOT * x for x in fields[0:3]] + list(fields[3:6])
    for f, value in enumerate(fields + [sound, 0.25 / LOG2E * rho, pressure, heavy]):
        other[f, spot, :] = value.reshape(CHIPS * TD, 128)


def fill_dummy(other):
    for f in range(9):
        other[f, OTHERS : OTHERS + 8, :] = jnp.zeros((8, 128), jnp.float32)
    other[9, OTHERS : OTHERS + 8, :] = jnp.full((8, 128), -1e30, jnp.float32)


def listing(codes, mine, twin, hits, listed, sem):
    core = lax.axis_index("core")
    own_rows = PAIRS // CAP
    hits[0:own_rows, :] = codes[...]
    place = lax.broadcasted_iota(jnp.int32, (CHIPS, 128), 0)
    for half, ref in enumerate((mine, twin)):
        got = ref[:, 72:80, :]
        named = jnp.where(core == 0, got[:, 0, :], got[:, 1, :])
        first = pltpu.roll(named, 128 - CAP, 1)
        code = (named.astype(jnp.int32) - 1) * SPAN + (half * CHIPS + place) * TD
        code = code + first.astype(jnp.int32)
        start = own_rows + half * CHIPS
        hits[start : start + CHIPS, :] = jnp.where(named > 0.5, code, OTHERS)
    copy = pltpu.make_async_copy(hits, listed, sem)
    copy.start()
    return copy


def advance(gain_rows, xs, vs):
    radius2 = xs[0] * xs[0] + xs[1] * xs[1] + xs[2] * xs[2] + SOFT
    pull = -STAR / (radius2 * jnp.sqrt(radius2))
    accel = [gain_rows[8 * k : 8 * k + 8, :] + pull * xs[k] for k in range(3)]
    speed = [vs[k] + DT * accel[k] for k in range(3)]
    place = [xs[k] + DT * speed[k] for k in range(3)]
    return accel, speed, place


def pairs_first(mine, twin, codes, ghost, pos, vel, mass, own, own_rest,
                new_pos, new_vel, accel, to_next, to_prev,
                other, gains, gain_rows, hits, listed, sem):
    copy = listing(codes, mine, twin, hits, listed, sem)
    xs = [pos[8 * k : 8 * k + 8, :] for k in range(3)]
    vs = [vel[8 * k : 8 * k + 8, :] for k in range(3)]
    for half, ref in enumerate((mine, twin)):
        fields = [ref[:, 8 * f : 8 * f + 8, :] for f in range(9)]
        fill_other(other, half, fields[0:6], fields[7], fields[8], fields[6])
    fill_dummy(other)
    copy.wait()
    pair_loop(listed, own, own_rest, other, gains)
    gathered_gain(gains, gain_rows)
    acc, speed, place = advance(gain_rows, xs, vs)
    for k in range(3):
        accel[8 * k : 8 * k + 8, :] = acc[k]
        new_vel[8 * k : 8 * k + 8, :] = speed[k]
        new_pos[8 * k : 8 * k + 8, :] = place[k]
    fill_outgoing(ghost, new_pos, mass, to_next, to_prev)


def pairs_second(mine, twin, mine_new, twin_new, codes, pos, vel, rho, own, own_rest,
                 out_pos, out_vel, out_accel, out_rho,
                 other, gains, gain_rows, hits, listed, sem):
    copy = listing(codes, mine, twin, hits, listed, sem)
    out_rho[...] = rho[...]
    for half, (ref, new) in enumerate(((mine, mine_new), (twin, twin_new))):
        old = [ref[:, 8 * f : 8 * f + 8, :] for f in range(8)]
        speed = [old[3 + k] + DT * new[:, 8 * k : 8 * k + 8, :] for k in range(3)]
        place = [old[k] + DT * speed[k] for k in range(3)]
        fill_other(other, half, place + speed, old[7], new[:, 24:32, :], old[6])
    fill_dummy(other)
    copy.wait()
    pair_loop(listed, own, own_rest, other, gains)
    gathered_gain(gains, gain_rows)
    xs = [pos[8 * k : 8 * k + 8, :] for k in range(3)]
    vs = [vel[8 * k : 8 * k + 8, :] for k in range(3)]
    acc, speed, place = advance(gain_rows, xs, vs)
    for k in range(3):
        for t in range(TD):
            span = slice(128 * t, 128 * t + 128)
            out_accel[k : k + 1, span] = acc[k][t : t + 1, :]
            out_vel[k : k + 1, span] = speed[k][t : t + 1, :]
            out_pos[k : k + 1, span] = place[k][t : t + 1, :]


def call(kernel, outs, ins, scratch=(), name=None):
    specs = [{"s": SMEM, "v": VMEM, "h": HBM}[spec] for spec in ins]
    return pl.pallas_call(
        kernel,
        out_shape=outs,
        in_specs=specs,
        out_specs=jax.tree.map(lambda _: VMEM, outs),
        scratch_shapes=scratch,
        compiler_params=pltpu.CompilerParams(vmem_limit_bytes=GRANT),
        name=name,
    )


def along_space(value, steps):
    count = lax.axis_size("space")
    return lax.ppermute(value, "space", [(i, (i + steps) % count) for i in range(count)])


def sector(value):
    mine = lax.all_to_all(value, "chip", 0, 0, tiled=True)
    return mine, lax.ppermute(mine, "core", [(0, 1), (1, 0)])


def local(positions, velocities, masses, sound2, ghost_list, dens_list, pair_dest, pair_tiles):
    pair_scratch = [
        pltpu.VMEM((10, OTHERS + 8, 128), jnp.float32),
        pltpu.VMEM((3 * TD, 128, 128), jnp.float32),
        pltpu.VMEM((3 * TD, 128), jnp.float32),
        pltpu.VMEM((PAIRS // CAP + 2 * CHIPS, 128), jnp.int32),
        pltpu.SMEM((PAIRS // CAP + 2 * CHIPS, 128), jnp.int32),
        pltpu.SemaphoreType.DMA,
    ]
    cand = [pltpu.VMEM((4 * (TD + 2 * G) + 8, 128), jnp.float32)]
    spread = [pltpu.VMEM((128, 128), jnp.float32)]
    ghost_rows = f32(4 * G, 128)
    places_shape = f32(3 * TD, 128, 128)
    rest_shape = f32(6 * TD, 128, 128)
    to_next, to_prev, codes, table, pos, vel, mass, snd, ghost, lists = call(
        begin_kernel,
        (
            ghost_rows,
            ghost_rows,
            i32(PAIRS // CAP, 128),
            f32(2 * CHIPS, 128),
            f32(24, 128),
            f32(24, 128),
            f32(TD, 128),
            f32(TD, 128),
            i32(2, G),
            i32(TD, NBD),
        ),
        "hhhhhhhh",
        scratch=[
            pltpu.VMEM((3, 128 * TD), jnp.float32),
            pltpu.VMEM((3, 128 * TD), jnp.float32),
            pltpu.VMEM((1, PAIRS), jnp.int32),
            pltpu.VMEM((2, PAIRS), jnp.int32),
            pltpu.SMEM((2, G), jnp.int32),
            pltpu.SemaphoreType.DMA((9,)),
        ],
        name="begin",
    )(
        *(
            pltpu.with_memory_space_constraint(value, pltpu.HBM)
            for value in (
                positions,
                velocities,
                masses.reshape(TD, 128),
                sound2.reshape(TD, 128),
                ghost_list.T,
                dens_list,
                pair_dest.T,
                pair_tiles.T,
            )
        )
    )
    below = along_space(to_next, 1)
    above = along_space(to_prev, -1)
    own = call(spread_places, places_shape, "v", scratch=spread, name="places_first")(pos)
    sent, rho = call(
        density_first,
        (f32(CHIPS, 80, 128), f32(TD, 128)),
        "vvvvvvsvv",
        scratch=cand,
        name="density_first",
    )(pos, vel, mass, snd, below, above, lists, table, own)
    mine, twin = sector(sent)
    rest = call(spread_rest, rest_shape, "vvv", scratch=spread, name="rest_first")(vel, snd, rho)
    new_pos, new_vel, accel, to_next, to_prev = call(
        pairs_first,
        (f32(24, 128), f32(24, 128), f32(24, 128), ghost_rows, ghost_rows),
        "vvvsvvvvv",
        scratch=pair_scratch,
        name="pairs_first",
    )(mine, twin, codes, ghost, pos, vel, mass, own, rest)
    below = along_space(to_next, 1)
    above = along_space(to_prev, -1)
    own = call(spread_places, places_shape, "v", scratch=spread, name="places_second")(new_pos)
    sent, rho = call(
        density_second,
        (f32(CHIPS, 32, 128), f32(TD, 128)),
        "vvvvvsv",
        scratch=cand,
        name="density_second",
    )(new_pos, mass, accel, below, above, lists, own)
    mine_new, twin_new = sector(sent)
    rest = call(spread_rest, rest_shape, "vvv", scratch=spread, name="rest_second")(
        new_vel, snd, rho
    )
    out_pos, out_vel, out_accel, out_rho = call(
        pairs_second,
        (f32(3, 1024), f32(3, 1024), f32(3, 1024), f32(TD, 128)),
        "vvvvvvvvvv",
        scratch=pair_scratch,
        name="pairs_second",
    )(mine, twin, mine_new, twin_new, codes, new_pos, new_vel, rho, own, rest)
    return (out_pos, out_vel, out_accel, out_rho.reshape(TD * 128))


def solution(mesh):
    grid = Mesh(mesh.devices.reshape(mesh.devices.shape[0], CHIPS, 2), ("space", "chip", "core"))
    every = ("space", "chip", "core")
    return jax.shard_map(
        local,
        mesh=grid,
        in_specs=(
            P(None, every),
            P(None, every),
            P(every),
            P(every),
            P(every, None),
            P(every, None),
            P(every, None),
            P(every, None),
        ),
        out_specs=(P(None, every), P(None, every), P(None, every), P(every)),
        check_vma=False,
    )
```

```python
import math

import jax
import jax.numpy as jnp
from jax import lax
from jax.experimental import pallas as pl
from jax.experimental.pallas import tpu as pltpu
from jax.sharding import Mesh, PartitionSpec as P

TD = 8
G = 4
NBD = 6
CAP = 4
PAIRS = 64
CHIPS = 16
OTHERS = 2 * CHIPS * TD
LOG2E = 1.4426950408889634
ROOT = LOG2E**0.5
STAR = 0.5
SOFT = 0.1
DT = 0.1
SPAN = 512
UNROLL = 16
GRANT = 16 * 1024 * 1024

VMEM = pl.BlockSpec(memory_space=pltpu.VMEM)
HBM = pl.BlockSpec(memory_space=pltpu.HBM)
SMEM = pl.BlockSpec(memory_space=pltpu.SMEM)


def f32(*shape):
    return jax.ShapeDtypeStruct(shape, jnp.float32)


def i32(*shape):
    return jax.ShapeDtypeStruct(shape, jnp.int32)


def begin_kernel(pos_in, vel_in, mass_in, sound2_in, ghost_in, lists_in, dest_in, tiles_in,
                 to_next, to_prev, codes, table, pos, vel, mass, sound2, ghost_out, lists,
                 wide_pos, wide_vel, dest, tiles, ghost, sems):
    moves = (
        (ghost_in, ghost),
        (pos_in, wide_pos),
        (mass_in, mass),
        (dest_in, dest),
        (tiles_in, tiles),
        (vel_in, wide_vel),
        (sound2_in, sound2),
        (lists_in, lists),
        (ghost_in, ghost_out),
    )
    copies = [pltpu.make_async_copy(src, dst, sems.at[n]) for n, (src, dst) in enumerate(moves)]
    for copy in copies:
        copy.start()
    for copy in copies:
        copy.wait()
    for t in range(TD):
        span = slice(128 * t, 128 * t + 128)
        for k in range(3):
            pos[8 * k + t : 8 * k + t + 1, :] = wide_pos[k : k + 1, span]
            vel[8 * k + t : 8 * k + t + 1, :] = wide_vel[k : k + 1, span]
    fill_outgoing(ghost, pos, mass, to_next, to_prev)
    core = lax.axis_index("core")
    d = dest[...]
    t0 = tiles[0:1, :]
    t1 = tiles[1:2, :]
    half = (d & 1) ^ core
    code = (t0 * SPAN + half * (CHIPS * TD) + (d >> 1) * TD + t1).astype(jnp.float32)
    row = lax.broadcasted_iota(jnp.int32, (PAIRS // CAP, PAIRS), 0)
    column = lax.broadcasted_iota(jnp.int32, (PAIRS // CAP, PAIRS), 1)
    lane = lax.broadcasted_iota(jnp.int32, (PAIRS // CAP, 128), 1)
    out = jnp.zeros((PAIRS // CAP, 128), jnp.float32)
    for c in range(CAP):
        chosen = jnp.where(column == CAP * row + c, code, 0.0)
        out = jnp.where(lane == c, jnp.sum(chosen, axis=1, keepdims=True), out)
    codes[...] = out.astype(jnp.int32)
    place = lax.broadcasted_iota(jnp.int32, (2 * CHIPS, PAIRS), 0)
    hits = (place == d).astype(jnp.float32)
    earlier = (
        lax.broadcasted_iota(jnp.int32, (PAIRS, PAIRS), 0)
        < lax.broadcasted_iota(jnp.int32, (PAIRS, PAIRS), 1)
    ).astype(jnp.float32)
    rank = jnp.dot(hits, earlier, preferred_element_type=jnp.float32)
    first = t0.astype(jnp.float32)
    second = t1.astype(jnp.float32) + 1.0
    lane = lax.broadcasted_iota(jnp.int32, (2 * CHIPS, 128), 1)
    out = jnp.zeros((2 * CHIPS, 128), jnp.float32)
    for c in range(CAP):
        chosen = jnp.where(rank == float(c), hits, 0.0)
        out = jnp.where(lane == c, jnp.sum(chosen * second, axis=1, keepdims=True), out)
        out = jnp.where(lane == CAP + c, jnp.sum(chosen * first, axis=1, keepdims=True), out)
    table[...] = out


def fill_outgoing(ghost, pos, mass, to_next, to_prev):
    for side, out in enumerate((to_next, to_prev)):
        for j in range(G):
            t = ghost[side, j]
            for k in range(3):
                out[4 * j + k : 4 * j + k + 1, :] = pos[pl.ds(8 * k + t, 1), :]
            out[4 * j + 3 : 4 * j + 4, :] = mass[pl.ds(t, 1), :]


def diagonal():
    sub = lax.broadcasted_iota(jnp.int32, (8, 128), 0)
    lane = lax.broadcasted_iota(jnp.int32, (8, 128), 1)
    return [lane == 8 * b + sub for b in range(16)]


def lane_sums(blocks, picks):
    total = jnp.zeros((8, 128), jnp.float32)
    for block, pick in zip(blocks, picks):
        total = jnp.where(pick, jnp.sum(block, axis=1, keepdims=True), total)
    return jnp.sum(total, axis=0, keepdims=True)


def spread_places(pos, own, rows):
    spread_tiles([pos[8 * k : 8 * k + 8, :] * ROOT for k in range(3)], own, rows)


def spread_rest(vel, sound2, rho, own, rows):
    fields = [vel[8 * k : 8 * k + 8, :] for k in range(3)]
    square = sound2[...]
    dense = rho[...]
    fields += [0.25 / ROOT * jnp.sqrt(square), 0.25 / LOG2E * dense, square / dense]
    spread_tiles(fields, own, rows)


def spread_tiles(fields, own, rows):
    count = len(fields)
    for f, value in enumerate(fields):
        for t in range(TD):
            rows[count * t + f : count * t + f + 1, :] = value[t : t + 1, :]
    rows[count * TD : 128, :] = jnp.zeros((128 - count * TD, 128), jnp.float32)
    columns = jnp.transpose(rows[...], (1, 0))
    for r in range(count * TD):
        own[r] = jnp.broadcast_to(columns[:, r : r + 1], (128, 128))


def density_of(cand, own, rho, lists):
    picks = diagonal()

    def tile(t):
        listed = [t] + [lists[t, c] for c in range(NBD)]
        other = [[cand[pl.ds(4 * j + k, 8, stride=0), :] for k in range(4)] for j in listed]
        blocks = []
        for b in range(16):
            rows = slice(8 * b, 8 * b + 8)
            xi, yi, zi = [own[3 * t + k, rows, :] for k in range(3)]
            total = None
            for xj, yj, zj, mj in other:
                dx = xi - xj
                dy = yi - yj
                dz = zi - zj
                part = jnp.exp2(mj - (dx * dx + dy * dy + dz * dz))
                total = part if total is None else total + part
            blocks.append(total)
        rho[pl.ds(t, 1), :] = lane_sums(blocks, picks)

    def one(n, carry):
        for u in range(4):
            tile(4 * n + u)
        return carry

    lax.fori_loop(0, TD // 4, one, 0)


def fill_ghosts(cand, below, above):
    row = lax.broadcasted_iota(jnp.int32, (4 * G, 128), 0)
    for start, ref in ((4 * TD, below), (4 * TD + 4 * G, above)):
        value = ref[...]
        value = jnp.where(row % 4 == 3, jnp.log2(jnp.where(row % 4 == 3, value, 1.0)), value * ROOT)
        cand[start : start + 4 * G, :] = value


def fill_candidates(cand, pos, heavy, below, above):
    for t in range(TD):
        for k in range(3):
            cand[4 * t + k : 4 * t + k + 1, :] = pos[8 * k + t : 8 * k + t + 1, :] * ROOT
        cand[4 * t + 3 : 4 * t + 4, :] = heavy[t : t + 1, :]
    fill_ghosts(cand, below, above)


def density_first(pos, vel, mass, sound2, below, above, lists, table, own, sent, density, cand):
    heavy = jnp.log2(mass[...])
    fill_candidates(cand, pos, heavy, below, above)
    density_of(cand, own, density, lists)
    places = pos[...]
    speeds = vel[...]
    sound = 0.25 / ROOT * jnp.sqrt(sound2[...])
    rho = density[...]
    for q in range(CHIPS):
        sent[q, 0:24, :] = places
        sent[q, 24:48, :] = speeds
        sent[q, 48:56, :] = heavy + (1.0 - math.log2(ROOT))
        sent[q, 56:64, :] = sound
        sent[q, 64:72, :] = rho
        sent[q, 72:80, :] = jnp.zeros((8, 128), jnp.float32)
        sent[q, 72:74, :] = table[2 * q : 2 * q + 2, :]


def density_second(pos, mass, accel, below, above, lists, own, sent, density, cand):
    fill_candidates(cand, pos, jnp.log2(mass[...]), below, above)
    density_of(cand, own, density, lists)
    moved = accel[...]
    rho = density[...]
    for q in range(CHIPS):
        sent[q, 0:24, :] = moved
        sent[q, 24:32, :] = rho


def pair_loop(listed, own, own_rest, other, gains):
    for r in range(3 * TD):
        gains[r] = jnp.zeros((128, 128), jnp.float32)

    def force(code):
        t = code >> 9
        place = t * 3
        rest = t * 6
        o = code & (SPAN - 1)
        xj, yj, zj, uj, vj, wj, sj, rj, pj, mj = [
            other[f, pl.ds(o, 8, stride=0), :] for f in range(10)
        ]
        for b in range(16):
            rows = slice(8 * b, 8 * b + 8)
            dx = own[place, rows, :] - xj
            dy = own[place + 1, rows, :] - yj
            dz = own[place + 2, rows, :] - zj
            d2 = dx * dx + dy * dy + dz * dz
            closing = (
                (own_rest[rest, rows, :] - uj) * dx
                + (own_rest[rest + 1, rows, :] - vj) * dy
                + (own_rest[rest + 2, rows, :] - wj) * dz
            )
            near = d2 + 0.01 * LOG2E
            closing = jnp.minimum(closing, 0.0) / near
            sound = own_rest[rest + 3, rows, :] + sj
            viscous = closing * (closing - sound) / (own_rest[rest + 4, rows, :] + rj)
            strength = own_rest[rest + 5, rows, :] + pj + viscous
            weight = strength * jnp.exp2(mj - d2)
            gains[place, rows, :] += weight * dx
            gains[place + 1, rows, :] += weight * dy
            gains[place + 2, rows, :] += weight * dz

    def one(n, carry):
        for u in range(UNROLL):
            force(listed[(UNROLL // CAP) * n + u // CAP, u % CAP])
        return carry

    lax.fori_loop(0, (PAIRS + 2 * CHIPS * CAP) // UNROLL, one, 0)


def gathered_gain(gains, gain_rows):
    picks = diagonal()
    for t in range(TD):
        for k in range(3):
            blocks = [gains[3 * t + k, 8 * b : 8 * b + 8, :] for b in range(16)]
            gain_rows[8 * k + t : 8 * k + t + 1, :] = lane_sums(blocks, picks)


def fill_other(other, half, fields, sound, rho, heavy):
    spot = slice(half * CHIPS * TD, (half + 1) * CHIPS * TD)
    pressure = 16.0 * LOG2E * sound * sound / rho
    fields = [ROOT * x for x in fields[0:3]] + list(fields[3:6])
    for f, value in enumerate(fields + [sound, 0.25 / LOG2E * rho, pressure, heavy]):
        other[f, spot, :] = value.reshape(CHIPS * TD, 128)


def fill_dummy(other):
    for f in range(9):
        other[f, OTHERS : OTHERS + 8, :] = jnp.zeros((8, 128), jnp.float32)
    other[9, OTHERS : OTHERS + 8, :] = jnp.full((8, 128), -1e30, jnp.float32)


def listing(codes, mine, twin, hits, listed, sem):
    core = lax.axis_index("core")
    own_rows = PAIRS // CAP
    hits[0:own_rows, :] = codes[...]
    place = lax.broadcasted_iota(jnp.int32, (CHIPS, 128), 0)
    for half, ref in enumerate((mine, twin)):
        got = ref[:, 72:80, :]
        named = jnp.where(core == 0, got[:, 0, :], got[:, 1, :])
        first = pltpu.roll(named, 128 - CAP, 1)
        code = (named.astype(jnp.int32) - 1) * SPAN + (half * CHIPS + place) * TD
        code = code + first.astype(jnp.int32)
        start = own_rows + half * CHIPS
        hits[start : start + CHIPS, :] = jnp.where(named > 0.5, code, OTHERS)
    copy = pltpu.make_async_copy(hits, listed, sem)
    copy.start()
    return copy


def advance(gain_rows, xs, vs):
    radius2 = xs[0] * xs[0] + xs[1] * xs[1] + xs[2] * xs[2] + SOFT
    pull = -STAR / (radius2 * jnp.sqrt(radius2))
    accel = [gain_rows[8 * k : 8 * k + 8, :] + pull * xs[k] for k in range(3)]
    speed = [vs[k] + DT * accel[k] for k in range(3)]
    place = [xs[k] + DT * speed[k] for k in range(3)]
    return accel, speed, place


def pairs_first(mine, twin, codes, ghost, pos, vel, mass, own, own_rest,
                new_pos, new_vel, accel, to_next, to_prev,
                other, gains, gain_rows, hits, listed, sem):
    copy = listing(codes, mine, twin, hits, listed, sem)
    xs = [pos[8 * k : 8 * k + 8, :] for k in range(3)]
    vs = [vel[8 * k : 8 * k + 8, :] for k in range(3)]
    for half, ref in enumerate((mine, twin)):
        fields = [ref[:, 8 * f : 8 * f + 8, :] for f in range(9)]
        fill_other(other, half, fields[0:6], fields[7], fields[8], fields[6])
    fill_dummy(other)
    copy.wait()
    pair_loop(listed, own, own_rest, other, gains)
    gathered_gain(gains, gain_rows)
    acc, speed, place = advance(gain_rows, xs, vs)
    for k in range(3):
        accel[8 * k : 8 * k + 8, :] = acc[k]
        new_vel[8 * k : 8 * k + 8, :] = speed[k]
        new_pos[8 * k : 8 * k + 8, :] = place[k]
    fill_outgoing(ghost, new_pos, mass, to_next, to_prev)


def pairs_second(mine, twin, mine_new, twin_new, codes, pos, vel, rho, own, own_rest,
                 out_pos, out_vel, out_accel, out_rho,
                 other, gains, gain_rows, hits, listed, sem):
    copy = listing(codes, mine, twin, hits, listed, sem)
    out_rho[...] = rho[...]
    for half, (ref, new) in enumerate(((mine, mine_new), (twin, twin_new))):
        old = [ref[:, 8 * f : 8 * f + 8, :] for f in range(8)]
        speed = [old[3 + k] + DT * new[:, 8 * k : 8 * k + 8, :] for k in range(3)]
        place = [old[k] + DT * speed[k] for k in range(3)]
        fill_other(other, half, place + speed, old[7], new[:, 24:32, :], old[6])
    fill_dummy(other)
    copy.wait()
    pair_loop(listed, own, own_rest, other, gains)
    gathered_gain(gains, gain_rows)
    xs = [pos[8 * k : 8 * k + 8, :] for k in range(3)]
    vs = [vel[8 * k : 8 * k + 8, :] for k in range(3)]
    acc, speed, place = advance(gain_rows, xs, vs)
    for k in range(3):
        for t in range(TD):
            span = slice(128 * t, 128 * t + 128)
            out_accel[k : k + 1, span] = acc[k][t : t + 1, :]
            out_vel[k : k + 1, span] = speed[k][t : t + 1, :]
            out_pos[k : k + 1, span] = place[k][t : t + 1, :]


def call(kernel, outs, ins, scratch=(), name=None):
    specs = [{"s": SMEM, "v": VMEM, "h": HBM}[spec] for spec in ins]
    return pl.pallas_call(
        kernel,
        out_shape=outs,
        in_specs=specs,
        out_specs=jax.tree.map(lambda _: VMEM, outs),
        scratch_shapes=scratch,
        compiler_params=pltpu.CompilerParams(vmem_limit_bytes=GRANT),
        name=name,
    )


def along_space(value, steps):
    count = lax.axis_size("space")
    return lax.ppermute(value, "space", [(i, (i + steps) % count) for i in range(count)])


def sector(value):
    mine = lax.all_to_all(value, "chip", 0, 0, tiled=True)
    return mine, lax.ppermute(mine, "core", [(0, 1), (1, 0)])


def local(positions, velocities, masses, sound2, ghost_list, dens_list, pair_dest, pair_tiles):
    pair_scratch = [
        pltpu.VMEM((10, OTHERS + 8, 128), jnp.float32),
        pltpu.VMEM((3 * TD, 128, 128), jnp.float32),
        pltpu.VMEM((3 * TD, 128), jnp.float32),
        pltpu.VMEM((PAIRS // CAP + 2 * CHIPS, 128), jnp.int32),
        pltpu.SMEM((PAIRS // CAP + 2 * CHIPS, 128), jnp.int32),
        pltpu.SemaphoreType.DMA,
    ]
    cand = [pltpu.VMEM((4 * (TD + 2 * G) + 8, 128), jnp.float32)]
    spread = [pltpu.VMEM((128, 128), jnp.float32)]
    ghost_rows = f32(4 * G, 128)
    places_shape = f32(3 * TD, 128, 128)
    rest_shape = f32(6 * TD, 128, 128)
    to_next, to_prev, codes, table, pos, vel, mass, snd, ghost, lists = call(
        begin_kernel,
        (
            ghost_rows,
            ghost_rows,
            i32(PAIRS // CAP, 128),
            f32(2 * CHIPS, 128),
            f32(24, 128),
            f32(24, 128),
            f32(TD, 128),
            f32(TD, 128),
            i32(2, G),
            i32(TD, NBD),
        ),
        "hhhhhhhh",
        scratch=[
            pltpu.VMEM((3, 128 * TD), jnp.float32),
            pltpu.VMEM((3, 128 * TD), jnp.float32),
            pltpu.VMEM((1, PAIRS), jnp.int32),
            pltpu.VMEM((2, PAIRS), jnp.int32),
            pltpu.SMEM((2, G), jnp.int32),
            pltpu.SemaphoreType.DMA((9,)),
        ],
        name="begin",
    )(
        *(
            pltpu.with_memory_space_constraint(value, pltpu.HBM)
            for value in (
                positions,
                velocities,
                masses.reshape(TD, 128),
                sound2.reshape(TD, 128),
                ghost_list.T,
                dens_list,
                pair_dest.T,
                pair_tiles.T,
            )
        )
    )
    below = along_space(to_next, 1)
    above = along_space(to_prev, -1)
    own = call(spread_places, places_shape, "v", scratch=spread, name="places_first")(pos)
    sent, rho = call(
        density_first,
        (f32(CHIPS, 80, 128), f32(TD, 128)),
        "vvvvvvsvv",
        scratch=cand,
        name="density_first",
    )(pos, vel, mass, snd, below, above, lists, table, own)
    mine, twin = sector(sent)
    rest = call(spread_rest, rest_shape, "vvv", scratch=spread, name="rest_first")(vel, snd, rho)
    new_pos, new_vel, accel, to_next, to_prev = call(
        pairs_first,
        (f32(24, 128), f32(24, 128), f32(24, 128), ghost_rows, ghost_rows),
        "vvvsvvvvv",
        scratch=pair_scratch,
        name="pairs_first",
    )(mine, twin, codes, ghost, pos, vel, mass, own, rest)
    below = along_space(to_next, 1)
    above = along_space(to_prev, -1)
    own = call(spread_places, places_shape, "v", scratch=spread, name="places_second")(new_pos)
    sent, rho = call(
        density_second,
        (f32(CHIPS, 32, 128), f32(TD, 128)),
        "vvvvvsv",
        scratch=cand,
        name="density_second",
    )(new_pos, mass, accel, below, above, lists, own)
    mine_new, twin_new = sector(sent)
    rest = call(spread_rest, rest_shape, "vvv", scratch=spread, name="rest_second")(
        new_vel, snd, rho
    )
    out_pos, out_vel, out_accel, out_rho = call(
        pairs_second,
        (f32(3, 1024), f32(3, 1024), f32(3, 1024), f32(TD, 128)),
        "vvvvvvvvvv",
        scratch=pair_scratch,
        name="pairs_second",
    )(mine, twin, mine_new, twin_new, codes, new_pos, new_vel, rho, own, rest)
    return (out_pos, out_vel, out_accel, out_rho.reshape(TD * 128))


def solution(mesh):
    grid = Mesh(mesh.devices.reshape(mesh.devices.shape[0], CHIPS, 2), ("space", "chip", "core"))
    every = ("space", "chip", "core")
    return jax.shard_map(
        local,
        mesh=grid,
        in_specs=(
            P(None, every),
            P(None, every),
            P(every),
            P(every),
            P(every, None),
            P(every, None),
            P(every, None),
            P(every, None),
        ),
        out_specs=(P(None, every), P(None, every), P(None, every), P(every)),
        check_vma=False,
    )
```
